512 devices in a mesh: blk: 128 (over y, z, x_lo), team: 4 (over x_hi, core).
Axes of the slice: x: 4 (x_hi: 2, x_lo: 2; x = x_hi * 2 + x_lo), y: 4, z: 16, core: 2. Of those that a mesh axis runs over, the one named last changes fastest.
Arguments:
- omega: float32 [128, 24, 128, 128], P('blk'), may hold values from -0.05 to 2, as said below
- dosage: float32 [128, 256, 128], P('blk', 'team'), may hold values from -6 to 6
- columns: int32 [128, 24], P('blk'), may hold values from 0 to 127, as said below
- counts: int32 [128], P('blk'), may hold values from 1 to 24, as said below
Outputs:
- new_omega: float32 [128, 24, 128, 128], P('blk')
- y_product: float32 [128, 256, 128], P('blk', 'team')
The draws below stay inside these ranges and needn't reach their ends.
Inputs may be any that keep to these rules, and one draw needn't show every extreme that they name: The first counts[b] slots of row b hold distinct block columns in ascending order, b among them; the pattern is symmetric (c is listed in row b exactly when b is listed in row c); every live column c of row b has |c - b| <= 8, or (c - b) mod 128 equal to f or 128 - f for one of the offsets f = 64 - j * 13, j = 0 to 3, and every row is linked at all these distant offsets; the other slots hold b. `counts`: some block row has exactly 24 in every draw. `omega`: symmetric: the block in row b for column c is the transpose of the block in row c for column b; diagonal entries of diagonal blocks lie in 1 to 2, all other entries in -0.05 to 0.05.
All inputs are finite; a program needn't handle non-finite values.
Results may differ from the reference program's by a relative error of at most 0.0003.
Values sent between devices are 32-bit elements; how exact they have to be, the bound alone decides.
No kernel may reach another device: no remote copies, remote signals or barrier semaphores. Data moves between devices by JAX's collectives and lax.ppermute only.
A program may use at most 64 MiB of HBM per device.

```python
import jax
import jax.numpy as jnp
from jax import lax

BLOCK = 128
ROWBLOCKS = 128
SAMPLES = 256
BAND = 8
FARLINKS = 4
FARSTEP = 13
SLOTS = 24


def link_pattern(key):
    base = jax.random.fold_in(key, 7)
    key_width, key_run = jax.random.split(base, 2)
    rolled = jax.random.randint(key_width, (ROWBLOCKS,), 0, BAND + 1)
    widths = rolled * rolled // BAND
    first = jax.random.randint(key_run, (), 0, ROWBLOCKS - 2 * BAND)
    rows = jnp.arange(ROWBLOCKS)
    inside = (rows >= first) & (rows <= first + 2 * BAND)
    widths = jnp.where(inside, BAND, widths)
    far = ROWBLOCKS // 2 - jnp.arange(FARLINKS) * FARSTEP
    offset = rows[None, :] - rows[:, None]
    near = jnp.abs(offset) <= jnp.minimum(widths[:, None], widths[None, :])
    wrapped = jnp.mod(offset, ROWBLOCKS)
    distant = jnp.any((wrapped[:, :, None] == far[None, None, :]) | (wrapped[:, :, None] == ROWBLOCKS - far[None, None, :]), axis=2)
    linked = near | distant
    link_counts = jnp.sum(linked, axis=1).astype(jnp.int32)
    ordered = jnp.sort(jnp.where(linked, rows[None, :], ROWBLOCKS + rows[None, :]), axis=1)[:, :SLOTS]
    link_columns = jnp.where(ordered >= ROWBLOCKS, rows[:, None], ordered).astype(jnp.int32)
    return (link_columns, link_counts)


def draw_columns(key, part):
    return link_pattern(key)[0]


def draw_counts(key, part):
    return link_pattern(key)[1]


def draw_omega(key, part):
    link_columns, link_counts = link_pattern(key)
    rows = jnp.broadcast_to(jnp.arange(ROWBLOCKS)[:, None], link_columns.shape)
    lower = jnp.minimum(rows, link_columns)
    upper = jnp.maximum(rows, link_columns)
    flipped = rows > link_columns
    base = jax.random.fold_in(key, 11)

    def one_block(low, high, flip):
        block_key = jax.random.fold_in(base, low * ROWBLOCKS + high)
        values = jnp.clip(jax.random.normal(block_key, (BLOCK, BLOCK), jnp.float32), -5.0, 5.0) * 0.01
        values = jnp.where(flip, values.T, values)
        mirrored = (values + values.T) * 0.5
        diag_values = jax.random.uniform(jax.random.fold_in(block_key, 1), (BLOCK,), jnp.float32, 1.0, 2.0)
        unit = jnp.eye(BLOCK, dtype=bool)
        diagonal_block = jnp.where(unit, diag_values[:, None], mirrored)
        return jnp.where(low == high, diagonal_block, values)
    return jax.vmap(jax.vmap(one_block))(lower, upper, flipped)


def steps_of(own_key, extent, pieces, low, high):
    def one(dim, blocks):
        heights = jax.random.uniform(jax.random.fold_in(jax.random.fold_in(own_key, 6), dim), (blocks,), jnp.float32, low / len(pieces), high / len(pieces))
        return jnp.repeat(jnp.exp(heights), extent[dim] // blocks).reshape((-1,) + (1,) * (len(extent) - dim - 1))

    loudness = one(*pieces[0])
    for cut in pieces[1:]:
        loudness = loudness * one(*cut)
    return loudness


def centred(stream_key, extent, spread, reach, shards=(), kind=jnp.bfloat16):
    entries = spread * jax.random.normal(stream_key, extent, jnp.float32)
    if shards:
        entries = entries * steps_of(stream_key, extent, shards, -0.22, 0.18)
    return jnp.clip(entries, -reach, reach).astype(kind)


def setup_inputs(seed: int = 0) -> dict:
    arg_keys = jax.random.split(jax.random.key(seed), 5)
    return {
        "omega": draw_omega(jax.random.fold_in(arg_keys[4], 71), 0),
        "dosage": centred(arg_keys[1], (ROWBLOCKS, SAMPLES, BLOCK), 1.0, 6.0, ((0, 128), (1, 4)), jnp.float32),
        "columns": draw_columns(jax.random.fold_in(arg_keys[4], 71), 0),
        "counts": draw_counts(jax.random.fold_in(arg_keys[4], 71), 0),
    }


step_size = 0.1
penalty = 0.05


def reference(omega, dosage, columns, counts):
    highest = lax.Precision.HIGHEST
    slot_ids = jnp.arange(SLOTS).astype(jnp.int32)
    live = slot_ids[None, :] < counts[:, None]
    row_ids = jnp.arange(ROWBLOCKS).astype(jnp.int32)

    def product_row(row):
        picked = jnp.where(live[row][:, None, None], dosage[columns[row]], 0.0)
        return jnp.einsum('ksb,kab->sa', picked, omega[row], precision=highest)

    y_product = lax.map(product_row, row_ids)
    unit = jnp.eye(BLOCK, dtype=bool)

    def update_row(row):
        keep = live[row]
        links = columns[row]
        far_dosage = jnp.where(keep[:, None, None], dosage[links], 0.0)
        far_product = jnp.where(keep[:, None, None], y_product[links], 0.0)
        grad = jnp.einsum('sa,ksb->kab', y_product[row], far_dosage, precision=highest)
        grad = grad + jnp.einsum('sa,ksb->kab', dosage[row], far_product, precision=highest)
        grad = grad / (2.0 * SAMPLES)
        on_diag = keep & (links == row)
        diag_values = jnp.sum(jnp.where(on_diag[:, None], jnp.diagonal(omega[row], axis1=1, axis2=2), 0.0), axis=0)
        corner = on_diag[:, None, None] & unit[None]
        grad = grad - jnp.where(corner, 1.0 / diag_values[None, None, :], 0.0)
        moved = omega[row] - step_size * grad
        shrunk = jnp.sign(moved) * jnp.maximum(jnp.abs(moved) - step_size * penalty, 0.0)
        result = jnp.where(corner, moved, shrunk)
        return jnp.where(keep[:, None, None], result, 0.0)

    new_omega = lax.map(update_row, row_ids)
    return new_omega, y_product
```

```python
import jax
import jax.numpy as jnp
import numpy as np
from jax import lax
from jax.sharding import PartitionSpec as P

step_size = 0.1
penalty = 0.05


AXES = ("blk", "team")
OFFSETS = np.array(
    [
        [1, 3, 5, 7, 38, 51],
        [-1, -3, -5, -7, -38, -51],
        [2, 4, 6, 8, 25, 64],
        [-2, -4, -6, -8, -25, 0],
    ]
)


def per_device(omega, dosage, columns, counts):
    weights = omega[0]
    own_dosage = dosage[0]
    links = columns[0]
    slot_count, block_size = weights.shape[:2]
    samples_here = own_dosage.shape[0]
    owner = lax.axis_index("blk")
    member = lax.axis_index("team")
    rows = lax.axis_size("blk")
    team = lax.axis_size("team")
    samples = samples_here * team
    rounds = OFFSETS.shape[1]
    precision = lax.Precision.HIGH

    def permute(x, target):
        pairs = []
        for b in range(rows):
            for t in range(team):
                b2, t2 = target(b, t)
                pairs.append((b * team + t, (b2 % rows) * team + t2))
        return lax.ppermute(x, AXES, pairs)

    live = jnp.arange(slot_count, dtype=jnp.int32) < counts[0]
    wrapped = jnp.mod(links - owner, rows)
    flat = np.mod(OFFSETS, rows).astype(np.int32)
    mine = jnp.asarray(flat)[member]
    match = (wrapped[None, :] == mine[:, None]) & live[None, :]
    have = jnp.any(match, axis=1)
    slot = jnp.argmax(match, axis=1).astype(jnp.int32)
    old = jnp.where(have[:, None, None], jnp.take(weights, slot, axis=0), 0.0)

    full = lax.all_gather(own_dosage, "team", axis=0, tiled=True)
    far = [
        permute(full, lambda b, t, k=k: (b - OFFSETS[t, k], t)) for k in range(rounds)
    ]
    far = jnp.stack(far)
    partial = jnp.einsum("ksb,kab->sa", far, old, precision=precision)
    partial = partial + permute(partial, lambda b, t: (b, t ^ 1))
    product = partial + permute(partial, lambda b, t: (b, t ^ 2))
    y_product = lax.dynamic_slice_in_dim(product, member * samples_here, samples_here, 0)

    send = jnp.einsum("kse,sa->kea", far, product, precision=precision)

    def back(t, k):
        return [u for u in range(team) if (OFFSETS[u, k] + OFFSETS[t, k]) % rows == 0][0]

    received = [
        permute(send[k], lambda b, t, k=k: (b + OFFSETS[t, k], back(t, k))) for k in range(rounds)
    ]
    local = jnp.einsum("sa,kse->kae", product, far, precision=precision)
    grad = (local + jnp.stack(received)) / (2.0 * samples)
    unit = jnp.eye(block_size, dtype=bool)
    corner = (mine == 0)[:, None, None] & unit[None]
    inverse = 1.0 / jnp.where(corner, old, 1.0)
    grad = grad - jnp.where(corner, inverse, 0.0)
    moved = old - step_size * grad
    shrunk = jnp.sign(moved) * jnp.maximum(jnp.abs(moved) - step_size * penalty, 0.0)
    tiles = jnp.where(corner, moved, shrunk)

    pair = jnp.concatenate([tiles, permute(tiles, lambda b, t: (b, t ^ 2))])
    every = jnp.concatenate([pair, permute(pair, lambda b, t: (b, t ^ 1))])
    order = jnp.asarray(np.array([0, 2, 1, 3], np.int32))
    same = wrapped[:, None, None] == jnp.asarray(flat)[None]
    place = order[member ^ jnp.arange(team, dtype=jnp.int32)][:, None] * rounds + jnp.arange(
        rounds, dtype=jnp.int32
    )
    position = jnp.sum(jnp.where(same, place[None], 0), axis=(1, 2))
    new_omega = jnp.where(live[:, None, None], jnp.take(every, position, axis=0), 0.0)
    return (new_omega[None], y_product[None])


def solution(mesh):
    return jax.shard_map(
        per_device,
        mesh=mesh,
        in_specs=(P("blk", None, None, None), P("blk", "team", None), P("blk", None), P("blk")),
        out_specs=(P("blk", None, None, None), P("blk", "team", None)),
        check_vma=False,
    )
```

```python
import jax
import jax.numpy as jnp
import numpy as np
from jax import lax
from jax.sharding import PartitionSpec as P

step_size = 0.1
penalty = 0.05


AXES = ("blk", "team")
NEAR_1, NEAR_2, SIDE_1, SIDE_2, FAR_1, FAR_2 = range(6)
PLACES = 6
OFFSETS = np.array(
    [
        [[2, 6, 3, 7, 38, 51], [-2, -6, -1, -5, -38, -51], [4, 8, 5, 0, 25, 1], [-4, -8, -3, -7, -25, 64]],
        [[2, 6, 1, 5, 38, 51], [-2, -6, -3, -7, -38, -51], [4, 8, 3, 7, 25, 64], [-4, -8, -5, 0, -25, -1]],
    ]
)


def per_device(omega, dosage, columns, counts):
    weights = omega[0]
    own_dosage = dosage[0]
    links = columns[0]
    slot_count, block_size = weights.shape[:2]
    samples_here = own_dosage.shape[0]
    owner = lax.axis_index("blk")
    member = lax.axis_index("team")
    rows = lax.axis_size("blk")
    team = lax.axis_size("team")
    samples = samples_here * team
    precision = lax.Precision.HIGH

    def permute(x, target):
        pairs = []
        for b in range(rows):
            for t in range(team):
                b2, t2 = target(b, t)
                pairs.append((b * team + t, (b2 % rows) * team + t2))
        return lax.ppermute(x, AXES, pairs)

    def partner(b, t, k):
        there = b + OFFSETS[b % 2, t, k]
        found = [
            u for u in range(team) if (OFFSETS[there % 2, u, k] + OFFSETS[b % 2, t, k]) % rows == 0
        ]
        return there, found[0]

    def fetch(x, k):
        source = {}
        for b in range(rows):
            for t in range(team):
                b2, t2 = partner(b, t, k)
                source[b2 % rows, t2] = (b, t)
        return permute(x, lambda b, t: source[b, t])

    live = jnp.arange(slot_count, dtype=jnp.int32) < counts[0]
    wrapped = jnp.mod(links - owner, rows)
    flat = jnp.asarray(np.mod(OFFSETS, rows).astype(np.int32))[owner % 2]
    mine = flat[member]
    match = (wrapped[None, :] == mine[:, None]) & live[None, :]
    have = jnp.any(match, axis=1)
    slot = jnp.argmax(match, axis=1).astype(jnp.int32)
    old = jnp.where(have[:, None, None], jnp.take(weights, slot, axis=0), 0.0)
    on_self = mine[SIDE_2] == 0

    full = lax.all_gather(own_dosage, "team", axis=0, tiled=True)
    column = [None] * PLACES
    for k in (FAR_2, NEAR_2, NEAR_1, FAR_1):
        column[k] = fetch(full, k)
    for k, near in ((SIDE_2, NEAR_2), (SIDE_1, NEAR_1)):
        column[k] = permute(column[near], lambda b, t: (b ^ 1, t))
    column[SIDE_2] = jnp.where(on_self, full, column[SIDE_2])

    partial = 0.0
    for k in (NEAR_2, NEAR_1, FAR_2, FAR_1, SIDE_2, SIDE_1):
        partial = partial + jnp.einsum("sb,ab->sa", column[k], old[k], precision=precision)
    partial = partial + permute(partial, lambda b, t: (b, t ^ 1))
    product = partial + permute(partial, lambda b, t: (b, t ^ 2))
    y_product = lax.dynamic_slice_in_dim(product, member * samples_here, samples_here, 0)

    def outgoing(k):
        return jnp.einsum("se,sa->ea", column[k], product, precision=precision)

    side = jnp.stack([outgoing(SIDE_1), outgoing(SIDE_2)])
    handed = permute(side, lambda b, t: (b ^ 1, t))
    received = [None] * PLACES
    for k in (FAR_2, FAR_1):
        received[k] = permute(outgoing(k), lambda b, t, k=k: partner(b, t, k))
    for k, at in ((NEAR_2, 1), (NEAR_1, 0)):
        both = permute(jnp.stack([outgoing(k), handed[at]]), lambda b, t, k=k: partner(b, t, k))
        received[k], received[k + 2] = both[0], both[1]
    received[SIDE_2] = jnp.where(on_self, side[1], received[SIDE_2])

    unit = jnp.eye(block_size, dtype=bool)
    tiles = []
    for k in range(PLACES):
        local = jnp.einsum("sa,se->ae", product, column[k], precision=precision)
        grad = (local + received[k]) / (2.0 * samples)
        if k == SIDE_2:
            corner = on_self & unit
            grad = grad - jnp.where(corner, 1.0 / jnp.where(corner, old[k], 1.0), 0.0)
        moved = old[k] - step_size * grad
        shrunk = jnp.sign(moved) * jnp.maximum(jnp.abs(moved) - step_size * penalty, 0.0)
        tiles.append(jnp.where(corner, moved, shrunk) if k == SIDE_2 else shrunk)
    tiles = jnp.stack(tiles)

    pair = jnp.concatenate([tiles, permute(tiles, lambda b, t: (b, t ^ 2))])
    every = jnp.concatenate([pair, permute(pair, lambda b, t: (b, t ^ 1))])
    order = jnp.asarray(np.array([0, 2, 1, 3], np.int32))
    same = wrapped[:, None, None] == flat[None]
    place = order[member ^ jnp.arange(team, dtype=jnp.int32)][:, None] * PLACES + jnp.arange(
        PLACES, dtype=jnp.int32
    )
    position = jnp.sum(jnp.where(same, place[None], 0), axis=(1, 2))
    new_omega = jnp.where(live[:, None, None], jnp.take(every, position, axis=0), 0.0)
    return (new_omega[None], y_product[None])


def solution(mesh):
    return jax.shard_map(
        per_device,
        mesh=mesh,
        in_specs=(P("blk", None, None, None), P("blk", "team", None), P("blk", None), P("blk")),
        out_specs=(P("blk", None, None, None), P("blk", "team", None)),
        check_vma=False,
    )
```

```python
import functools

import jax
import jax.numpy as jnp
import numpy as np
from jax import lax
from jax.experimental import pallas as pl
from jax.experimental.pallas import tpu as pltpu
from jax.sharding import PartitionSpec as P


step_size = 0.1
penalty = 0.05


AXES = ("blk", "team")
NEAR_1, NEAR_2, SIDE_1, SIDE_2, FAR_1, FAR_2 = range(6)
PLACES = 6
OFFSETS = np.array(
    [
        [[2, 6, 3, 7, 38, 51], [-2, -6, -1, -5, -38, -51], [4, 8, 5, 0, 25, 1], [-4, -8, -3, -7, -25, 64]],
        [[2, 6, 1, 5, 38, 51], [-2, -6, -3, -7, -38, -51], [4, 8, 3, 7, 25, 64], [-4, -8, -5, 0, -25, -1]],
    ]
)
VMEM = pl.BlockSpec(memory_space=pltpu.VMEM)
SMEM = pl.BlockSpec(memory_space=pltpu.SMEM)
HBM = pl.BlockSpec(memory_space=pltpu.MemorySpace.HBM)


def split(x):
    high = x.astype(jnp.bfloat16)
    return high, (x - high.astype(jnp.float32)).astype(jnp.bfloat16)


def dot3(a, b, dims):
    def one(x, y):
        return lax.dot_general(x, y, (dims, ((), ())), preferred_element_type=jnp.float32)

    return one(a[0], b[0]) + (one(a[0], b[1]) + one(a[1], b[0]))


def pick_kernel(table, ids, columns, counts, omega, slots, old, sems):
    owner, member = ids[0], ids[1]
    count = counts[0]
    parity = lax.rem(owner, 2)
    total = table.shape[1]
    slot_count = columns.shape[1]
    for i in range(total):
        slots[i] = -1

    def match(s, carry):
        offset = lax.rem(columns[0, s] - owner + 128, 128)
        for i in range(total):

            @pl.when(table[parity, i] == offset)
            def _():
                slots[i] = s

        return carry

    lax.fori_loop(0, jnp.minimum(count, slot_count), match, 0)
    for k in range(PLACES):
        slot = slots[member * PLACES + k]

        @pl.when(slot >= 0)
        def _():
            pltpu.make_async_copy(omega.at[slot], old.at[k], sems.at[k]).start()

        @pl.when(slot < 0)
        def _():
            old[k] = jnp.zeros(old.shape[1:], jnp.float32)

    for k in range(PLACES):
        slot = slots[member * PLACES + k]

        @pl.when(slot >= 0)
        def _():
            pltpu.make_async_copy(omega.at[slot], old.at[k], sems.at[k]).wait()


def partial_kernel(own_side, old, full, *refs):
    column, out = refs[:PLACES], refs[PLACES]
    total = jnp.zeros(out.shape, jnp.float32)
    for k in range(PLACES):
        x = column[k][...]
        if k == SIDE_2:
            x = jnp.where(own_side[0] == 1, full[...], x)
        total = total + dot3(split(x), split(old[k]), ((1,), (1,)))
    out[...] = total


def tile_kernel(own_side, ids, half, other, full, *refs):
    column = refs[:PLACES]
    near_1, near_2, side, far_1, far_2, y_out = refs[PLACES:]
    product = half[...] + other[...]
    samples_here = y_out.shape[0]
    turned = split(product.T)
    for k in range(PLACES):
        x = column[k][...]
        if k == SIDE_2:
            x = jnp.where(own_side[0] == 1, full[...], x)
        tile = dot3(turned, split(x), ((1,), (0,)))
        if k in (SIDE_1, SIDE_2):
            side[k - SIDE_1] = tile
        else:
            {NEAR_1: near_1, NEAR_2: near_2, FAR_1: far_1, FAR_2: far_2}[k][...] = tile
    start = pl.multiple_of(ids[1] * samples_here, samples_here)
    y_out[...] = half[pl.ds(start, samples_here), :] + other[pl.ds(start, samples_here), :]


def update_kernel(samples, own_side, old, near_1, near_2, side, far_1, far_2, got_1, got_2, got_far_1, got_far_2, out):
    on_self = own_side[0] == 1
    shape = out.shape[1:]
    unit = lax.broadcasted_iota(jnp.int32, shape, 0) == lax.broadcasted_iota(jnp.int32, shape, 1)
    local = [near_1[...], near_2[...], side[0], side[1], far_1[...], far_2[...]]
    given = [got_1[0], got_2[0], got_1[1], got_2[1], got_far_1[...], got_far_2[...]]
    for k in range(PLACES):
        before = old[k]
        theirs = given[k]
        if k == SIDE_2:
            theirs = jnp.where(on_self, local[k], theirs)
        grad = (local[k] + theirs.T) / (2.0 * samples)
        if k == SIDE_2:
            corner = jnp.logical_and(unit, on_self)
            grad = grad - jnp.where(corner, 1.0 / jnp.where(corner, before, 1.0), 0.0)
        moved = before - step_size * grad
        size = jnp.maximum(jnp.abs(moved) - step_size * penalty, 0.0)
        shrunk = jnp.where(moved < 0.0, -size, size)
        out[k] = jnp.where(corner, moved, shrunk) if k == SIDE_2 else shrunk


def copies(groups, slots, ids, out, sems):
    found = []
    for n, (j, tiles) in enumerate(groups):
        for k in range(PLACES):
            slot = slots[lax.bitwise_xor(ids[1], j) * PLACES + k]
            target = jnp.maximum(slot, 0)
            found.append((slot >= 0, pltpu.make_async_copy(tiles.at[k], out.at[target], sems.at[n * PLACES + k])))
    return found


def place_kernel(which, slots, ids, counts, *refs):
    if which == 0:
        groups, (out, zero, sems, zero_sem) = list(zip((0, 1, 2), refs[:3])), refs[3:]
    else:
        groups, (out, sems) = [(3, refs[0])], refs[2:]
    found = copies(groups, slots, ids, out, sems)
    for condition, copy in found:
        pl.when(condition)(copy.start)
    if which == 0:
        zero[...] = jnp.zeros(zero.shape, jnp.float32)
        slot_count = out.shape[0]
        first = jnp.clip(counts[0], 0, slot_count)

        @pl.loop(first, slot_count)
        def _(s):
            pltpu.make_async_copy(zero, out.at[s], zero_sem).start()
            pltpu.make_async_copy(zero, out.at[s], zero_sem).wait()

    for condition, copy in found:
        pl.when(condition)(copy.wait)


PARAMS = pltpu.CompilerParams(vmem_limit_bytes=8 * 2**20)


def cost(flops, nbytes):
    return pl.CostEstimate(flops=flops, bytes_accessed=nbytes, transcendentals=0)


def step(omega, dosage, columns, counts):
    weights = omega[0]
    own_dosage = dosage[0]
    slot_count, block_size = weights.shape[:2]
    samples_here = own_dosage.shape[0]
    owner = lax.axis_index("blk")
    member = lax.axis_index("team")
    rows = lax.axis_size("blk")
    team = lax.axis_size("team")
    samples = samples_here * team
    f32 = jnp.float32

    def permute(x, target):
        pairs = []
        for b in range(rows):
            for t in range(team):
                b2, t2 = target(b, t)
                pairs.append((b * team + t, (b2 % rows) * team + t2))
        return lax.ppermute(x, AXES, pairs)

    def partner(b, t, k):
        there = b + OFFSETS[b % 2, t, k]
        found = [
            u for u in range(team) if (OFFSETS[there % 2, u, k] + OFFSETS[b % 2, t, k]) % rows == 0
        ]
        return there, found[0]

    def fetch(x, k):
        source = {}
        for b in range(rows):
            for t in range(team):
                b2, t2 = partner(b, t, k)
                source[b2 % rows, t2] = (b, t)
        return permute(x, lambda b, t: source[b, t])

    def beside(b, t):
        return b ^ 1, t

    ids = jnp.stack([owner, member]).astype(jnp.int32)
    own_side = jnp.logical_or(
        jnp.logical_and(owner % 2 == 0, member == 2), jnp.logical_and(owner % 2 == 1, member == 3)
    ).astype(jnp.int32)[None]
    table = jnp.asarray(np.mod(OFFSETS, rows).astype(np.int32).reshape(2, team * PLACES))
    tile_shape = jax.ShapeDtypeStruct((block_size, block_size), f32)
    tiles_shape = jax.ShapeDtypeStruct((PLACES, block_size, block_size), f32)
    tile_bytes = block_size * block_size * 4

    slots, old = pl.pallas_call(
        pick_kernel,
        name="pick",
        out_shape=(jax.ShapeDtypeStruct((team * PLACES,), jnp.int32), tiles_shape),
        in_specs=[SMEM, SMEM, SMEM, SMEM, HBM],
        out_specs=(SMEM, VMEM),
        scratch_shapes=[pltpu.SemaphoreType.DMA((PLACES,))],
        compiler_params=PARAMS,
        cost_estimate=cost(0, 2 * PLACES * tile_bytes),
    )(table, ids, columns, counts, weights)

    full = lax.all_gather(own_dosage, "team", axis=0, tiled=True)
    column = [None] * PLACES
    column[FAR_2] = fetch(full, FAR_2)
    column[NEAR_2] = fetch(full, NEAR_2)
    column[NEAR_1] = fetch(full, NEAR_1)
    column[FAR_1] = fetch(full, FAR_1)
    column[SIDE_2] = permute(column[NEAR_2], beside)
    column[SIDE_1] = permute(column[NEAR_1], beside)

    partial = pl.pallas_call(
        partial_kernel,
        name="partial",
        out_shape=jax.ShapeDtypeStruct((samples, block_size), f32),
        in_specs=[SMEM] + [VMEM] * (2 + PLACES),
        out_specs=VMEM,
        compiler_params=PARAMS,
        cost_estimate=cost(2 * PLACES * samples * block_size**2, 14 * samples * block_size * 4),
    )(own_side, old, full, *column)
    half = partial + permute(partial, lambda b, t: (b, t ^ 1))
    other = permute(half, lambda b, t: (b, t ^ 2))

    near_1, near_2, side, far_1, far_2, y_product = pl.pallas_call(
        tile_kernel,
        name="tiles",
        out_shape=(
            tile_shape,
            tile_shape,
            jax.ShapeDtypeStruct((2, block_size, block_size), f32),
            tile_shape,
            tile_shape,
            jax.ShapeDtypeStruct((samples_here, block_size), f32),
        ),
        in_specs=[SMEM, SMEM] + [VMEM] * (3 + PLACES),
        out_specs=(VMEM,) * 6,
        compiler_params=PARAMS,
        cost_estimate=cost(2 * PLACES * samples * block_size**2, 14 * samples * block_size * 4),
    )(own_side, ids, half, other, full, *column)

    handed = permute(side, beside)

    def back(x, k):
        return permute(x, lambda b, t: partner(b, t, k))

    got_far_2 = back(far_2, FAR_2)
    got_far_1 = back(far_1, FAR_1)
    got_2 = back(jnp.stack([near_2, handed[1]]), NEAR_2)
    got_1 = back(jnp.stack([near_1, handed[0]]), NEAR_1)

    tiles = pl.pallas_call(
        functools.partial(update_kernel, samples),
        name="update",
        out_shape=tiles_shape,
        in_specs=[SMEM] + [VMEM] * 10,
        out_specs=VMEM,
        compiler_params=PARAMS,
        cost_estimate=cost(0, 4 * PLACES * tile_bytes),
    )(own_side, old, near_1, near_2, side, far_1, far_2, got_1, got_2, got_far_1, got_far_2)

    across = permute(tiles, lambda b, t: (b, t ^ 2))
    mate = permute(tiles, lambda b, t: (b, t ^ 1))
    last = permute(across, lambda b, t: (b, t ^ 1))
    out_shape = jax.ShapeDtypeStruct((slot_count, block_size, block_size), f32)
    new_omega = pl.pallas_call(
        functools.partial(place_kernel, 0),
        name="place_1",
        out_shape=out_shape,
        in_specs=[SMEM] * 3 + [VMEM] * 3,
        out_specs=HBM,
        scratch_shapes=[
            pltpu.VMEM((block_size, block_size), f32),
            pltpu.SemaphoreType.DMA((3 * PLACES,)),
            pltpu.SemaphoreType.DMA,
        ],
        compiler_params=PARAMS,
        cost_estimate=cost(0, 6 * PLACES * tile_bytes),
    )(slots, ids, counts, tiles, mate, across)
    new_omega = pl.pallas_call(
        functools.partial(place_kernel, 1),
        name="place_2",
        out_shape=out_shape,
        in_specs=[SMEM] * 3 + [VMEM, HBM],
        out_specs=HBM,
        input_output_aliases={4: 0},
        scratch_shapes=[pltpu.SemaphoreType.DMA((PLACES,))],
        compiler_params=PARAMS,
        cost_estimate=cost(0, 2 * PLACES * tile_bytes),
    )(slots, ids, counts, last, new_omega)
    return (new_omega[None], y_product[None])


def solution(mesh):
    return jax.shard_map(
        step,
        mesh=mesh,
        in_specs=(P("blk", None, None, None), P("blk", "team", None), P("blk", None), P("blk")),
        out_specs=(P("blk", None, None, None), P("blk", "team", None)),
        check_vma=False,
    )
```

```python
import functools

import jax
import jax.numpy as jnp
import numpy as np
from jax import lax
from jax.experimental import pallas as pl
from jax.experimental.pallas import tpu as pltpu
from jax.sharding import PartitionSpec as P


step_size = 0.1
penalty = 0.05


AXES = ("blk", "team")
NEAR_1, NEAR_2, SIDE_1, SIDE_2, FAR_1, FAR_2 = range(6)
PLACES = 6
OFFSETS = np.array(
    [
        [[2, 4, 3, 5, 38, 51], [-2, -4, -1, -3, -38, -51], [6, 8, 7, 0, 25, 1], [-6, -8, -5, -7, -25, 64]],
        [[2, 4, 1, 3, 38, 51], [-2, -4, -3, -5, -38, -51], [6, 8, 5, 7, 25, 64], [-6, -8, -7, 0, -25, -1]],
    ]
)
VMEM = pl.BlockSpec(memory_space=pltpu.VMEM)
SMEM = pl.BlockSpec(memory_space=pltpu.SMEM)
HBM = pl.BlockSpec(memory_space=pltpu.MemorySpace.HBM)


def split(x):
    high = x.astype(jnp.bfloat16)
    return high, (x - high.astype(jnp.float32)).astype(jnp.bfloat16)


def dot3(a, b, dims):
    def one(x, y):
        return lax.dot_general(x, y, (dims, ((), ())), preferred_element_type=jnp.float32)

    return one(a[0], b[0]) + (one(a[0], b[1]) + one(a[1], b[0]))


def pick_kernel(table, ids, columns, counts, omega, slots, old, sems):
    owner, member = ids[0], ids[1]
    count = counts[0]
    parity = lax.rem(owner, 2)
    total = table.shape[1]
    slot_count = columns.shape[1]
    for i in range(total):
        slots[i] = -1

    def match(s, carry):
        offset = lax.rem(columns[0, s] - owner + 128, 128)
        for i in range(total):

            @pl.when(table[parity, i] == offset)
            def _():
                slots[i] = s

        return carry

    lax.fori_loop(0, jnp.minimum(count, slot_count), match, 0)
    for k in range(PLACES):
        slot = slots[member * PLACES + k]

        @pl.when(slot >= 0)
        def _():
            pltpu.make_async_copy(omega.at[slot], old.at[k], sems.at[k]).start()

        @pl.when(slot < 0)
        def _():
            old[k] = jnp.zeros(old.shape[1:], jnp.float32)

    for k in range(PLACES):
        slot = slots[member * PLACES + k]

        @pl.when(slot >= 0)
        def _():
            pltpu.make_async_copy(omega.at[slot], old.at[k], sems.at[k]).wait()


def partial_kernel(own_side, old, full, *refs):
    column, out = refs[:PLACES], refs[PLACES]
    total = jnp.zeros(out.shape, jnp.float32)
    for k in range(PLACES):
        x = column[k][...]
        if k == SIDE_2:
            x = jnp.where(own_side[0] == 1, full[...], x)
        total = total + dot3(split(x), split(old[k]), ((1,), (1,)))
    out[...] = total


def tile_kernel(own_side, ids, half, other, full, *refs):
    column = refs[:PLACES]
    near_1, near_2, side, far_1, far_2, y_out = refs[PLACES:]
    product = half[...] + other[...]
    samples_here = y_out.shape[0]
    turned = split(product.T)
    for k in range(PLACES):
        x = column[k][...]
        if k == SIDE_2:
            x = jnp.where(own_side[0] == 1, full[...], x)
        tile = dot3(turned, split(x), ((1,), (0,)))
        if k in (SIDE_1, SIDE_2):
            side[k - SIDE_1] = tile
        else:
            {NEAR_1: near_1, NEAR_2: near_2, FAR_1: far_1, FAR_2: far_2}[k][...] = tile
    start = pl.multiple_of(ids[1] * samples_here, samples_here)
    y_out[...] = half[pl.ds(start, samples_here), :] + other[pl.ds(start, samples_here), :]


def update(before, ours, theirs, samples, corner=None):
    grad = (ours + theirs.T) / (2.0 * samples)
    if corner is not None:
        grad = grad - jnp.where(corner, 1.0 / jnp.where(corner, before, 1.0), 0.0)
    moved = before - step_size * grad
    size = jnp.maximum(jnp.abs(moved) - step_size * penalty, 0.0)
    shrunk = jnp.where(moved < 0.0, -size, size)
    return shrunk if corner is None else jnp.where(corner, moved, shrunk)


def update_far_kernel(samples, old, far_1, far_2, got_1, got_2, out):
    out[0] = update(old[FAR_1], far_1[...], got_1[...], samples)
    out[1] = update(old[FAR_2], far_2[...], got_2[...], samples)


def update_near_kernel(samples, own_side, old, near_1, near_2, side, got_1, got_2, out):
    on_self = own_side[0] == 1
    shape = out.shape[1:]
    unit = lax.broadcasted_iota(jnp.int32, shape, 0) == lax.broadcasted_iota(jnp.int32, shape, 1)
    out[NEAR_1] = update(old[NEAR_1], near_1[...], got_1[0], samples)
    out[NEAR_2] = update(old[NEAR_2], near_2[...], got_2[0], samples)
    out[SIDE_1] = update(old[SIDE_1], side[0], got_1[1], samples)
    theirs = jnp.where(on_self, side[1], got_2[1])
    out[SIDE_2] = update(old[SIDE_2], side[1], theirs, samples, jnp.logical_and(unit, on_self))


NEAR_PLACES = (NEAR_1, NEAR_2, SIDE_1, SIDE_2)
FAR_PLACES = (FAR_1, FAR_2)


def place_kernel(groups, places, fill, slots, ids, counts, *refs):
    n = len(groups)
    if fill:
        out, zero, sems, zero_sems = refs[n:]
    else:
        out, sems = refs[n + 1 :]
    found = []
    for g, j in enumerate(groups):
        for i, k in enumerate(places):
            slot = slots[lax.bitwise_xor(ids[1], j) * PLACES + k]
            copy = pltpu.make_async_copy(
                refs[g].at[i], out.at[jnp.maximum(slot, 0)], sems.at[g * len(places) + i]
            )
            found.append((slot >= 0, copy))
    for condition, copy in found:
        pl.when(condition)(copy.start)
    if fill:
        zero[...] = jnp.zeros(zero.shape, jnp.float32)
        slot_count = out.shape[0]
        first = jnp.clip(counts[0], 0, slot_count)

        @pl.loop(first, slot_count)
        def _(s):
            pltpu.make_async_copy(zero, out.at[s], zero_sems.at[s]).start()

        @pl.loop(first, slot_count)
        def _(s):
            pltpu.make_async_copy(zero, out.at[s], zero_sems.at[s]).wait()

    for condition, copy in found:
        pl.when(condition)(copy.wait)


PARAMS = pltpu.CompilerParams(vmem_limit_bytes=8 * 2**20)


def cost(flops, nbytes):
    return pl.CostEstimate(flops=flops, bytes_accessed=nbytes, transcendentals=0)


def step(omega, dosage, columns, counts):
    weights = omega[0]
    own_dosage = dosage[0]
    slot_count, block_size = weights.shape[:2]
    samples_here = own_dosage.shape[0]
    owner = lax.axis_index("blk")
    member = lax.axis_index("team")
    rows = lax.axis_size("blk")
    team = lax.axis_size("team")
    samples = samples_here * team
    f32 = jnp.float32

    def permute(x, target):
        pairs = []
        for b in range(rows):
            for t in range(team):
                b2, t2 = target(b, t)
                pairs.append((b * team + t, (b2 % rows) * team + t2))
        return lax.ppermute(x, AXES, pairs)

    def partner(b, t, k):
        there = b + OFFSETS[b % 2, t, k]
        found = [
            u for u in range(team) if (OFFSETS[there % 2, u, k] + OFFSETS[b % 2, t, k]) % rows == 0
        ]
        return there, found[0]

    def fetch(x, k):
        source = {}
        for b in range(rows):
            for t in range(team):
                b2, t2 = partner(b, t, k)
                source[b2 % rows, t2] = (b, t)
        return permute(x, lambda b, t: source[b, t])

    def beside(b, t):
        return b ^ 1, t

    ids = jnp.stack([owner, member]).astype(jnp.int32)
    own_side = jnp.logical_or(
        jnp.logical_and(owner % 2 == 0, member == 2), jnp.logical_and(owner % 2 == 1, member == 3)
    ).astype(jnp.int32)[None]
    table = jnp.asarray(np.mod(OFFSETS, rows).astype(np.int32).reshape(2, team * PLACES))
    tile_shape = jax.ShapeDtypeStruct((block_size, block_size), f32)
    tiles_shape = jax.ShapeDtypeStruct((PLACES, block_size, block_size), f32)
    tile_bytes = block_size * block_size * 4

    slots, old = pl.pallas_call(
        pick_kernel,
        name="pick",
        out_shape=(jax.ShapeDtypeStruct((team * PLACES,), jnp.int32), tiles_shape),
        in_specs=[SMEM, SMEM, SMEM, SMEM, HBM],
        out_specs=(SMEM, VMEM),
        scratch_shapes=[pltpu.SemaphoreType.DMA((PLACES,))],
        compiler_params=PARAMS,
        cost_estimate=cost(0, 2 * PLACES * tile_bytes),
    )(table, ids, columns, counts, weights)

    full = lax.all_gather(own_dosage, "team", axis=0, tiled=True)
    column = [None] * PLACES
    column[FAR_2] = fetch(full, FAR_2)
    column[NEAR_2] = fetch(full, NEAR_2)
    column[NEAR_1] = fetch(full, NEAR_1)
    column[FAR_1] = fetch(full, FAR_1)
    column[SIDE_2] = permute(column[NEAR_2], beside)
    column[SIDE_1] = permute(column[NEAR_1], beside)

    partial = pl.pallas_call(
        partial_kernel,
        name="partial",
        out_shape=jax.ShapeDtypeStruct((samples, block_size), f32),
        in_specs=[SMEM] + [VMEM] * (2 + PLACES),
        out_specs=VMEM,
        compiler_params=PARAMS,
        cost_estimate=cost(2 * PLACES * samples * block_size**2, 14 * samples * block_size * 4),
    )(own_side, old, full, *column)
    half = partial + permute(partial, lambda b, t: (b, t ^ 1))
    other = permute(half, lambda b, t: (b, t ^ 2))

    near_1, near_2, side, far_1, far_2, y_product = pl.pallas_call(
        tile_kernel,
        name="tiles",
        out_shape=(
            tile_shape,
            tile_shape,
            jax.ShapeDtypeStruct((2, block_size, block_size), f32),
            tile_shape,
            tile_shape,
            jax.ShapeDtypeStruct((samples_here, block_size), f32),
        ),
        in_specs=[SMEM, SMEM] + [VMEM] * (3 + PLACES),
        out_specs=(VMEM,) * 6,
        compiler_params=PARAMS,
        cost_estimate=cost(2 * PLACES * samples * block_size**2, 14 * samples * block_size * 4),
    )(own_side, ids, half, other, full, *column)

    handed = permute(side, beside)

    def back(x, k):
        return permute(x, lambda b, t: partner(b, t, k))

    got_far_2 = back(far_2, FAR_2)
    got_far_1 = back(far_1, FAR_1)
    got_2 = back(jnp.stack([near_2, handed[1]]), NEAR_2)
    got_1 = back(jnp.stack([near_1, handed[0]]), NEAR_1)

    def kernel(function, out_shape, in_specs, nbytes):
        return pl.pallas_call(
            function,
            out_shape=out_shape,
            in_specs=in_specs,
            out_specs=VMEM,
            compiler_params=PARAMS,
            cost_estimate=cost(0, nbytes),
        )

    def tiles_of(count):
        return jax.ShapeDtypeStruct((count, block_size, block_size), f32)

    far_tiles = kernel(
        functools.partial(update_far_kernel, samples), tiles_of(2), [VMEM] * 5, 8 * tile_bytes
    )(old, far_1, far_2, got_far_1, got_far_2)
    near_tiles = kernel(
        functools.partial(update_near_kernel, samples), tiles_of(4), [SMEM] + [VMEM] * 6, 16 * tile_bytes
    )(own_side, old, near_1, near_2, side, got_1, got_2)

    def chip(b, t):
        return b, t ^ 2

    def core(b, t):
        return b, t ^ 1

    far_across = permute(far_tiles, chip)
    far_mate = permute(far_tiles, core)
    near_across = permute(near_tiles, chip)
    near_mate = permute(near_tiles, core)
    far_last = permute(far_across, core)
    near_last = permute(near_across, core)

    def place(groups, places, tiles, into):
        fill = into is None
        n = len(groups)
        sems = [pltpu.SemaphoreType.DMA((n * len(places),))]
        if fill:
            scratch = [pltpu.VMEM((block_size, block_size), f32)] + sems + [pltpu.SemaphoreType.DMA((slot_count,))]
        else:
            scratch = sems
        return pl.pallas_call(
            functools.partial(place_kernel, groups, places, fill),
            out_shape=tiles_of(slot_count),
            in_specs=[SMEM] * 3 + [VMEM] * n + ([] if fill else [HBM]),
            out_specs=HBM,
            input_output_aliases={} if fill else {3 + n: 0},
            scratch_shapes=scratch,
            compiler_params=PARAMS,
            cost_estimate=cost(0, 2 * n * len(places) * tile_bytes),
        )(slots, ids, counts, *tiles, *([] if fill else [into]))

    new_omega = place((0, 1, 2, 3), FAR_PLACES, (far_tiles, far_mate, far_across, far_last), None)
    new_omega = place((0, 1, 2), NEAR_PLACES, (near_tiles, near_mate, near_across), new_omega)
    new_omega = place((3,), NEAR_PLACES, (near_last,), new_omega)
    return (new_omega[None], y_product[None])


def solution(mesh):
    return jax.shard_map(
        step,
        mesh=mesh,
        in_specs=(P("blk", None, None, None), P("blk", "team", None), P("blk", None), P("blk")),
        out_specs=(P("blk", None, None, None), P("blk", "team", None)),
        check_vma=False,
    )
```

```python
import functools

import jax
import jax.numpy as jnp
import numpy as np
from jax import lax
from jax.experimental import pallas as pl
from jax.experimental.pallas import tpu as pltpu
from jax.sharding import PartitionSpec as P


step_size = 0.1
penalty = 0.05


AXES = ("blk", "team")
NEAR_1, NEAR_2, SIDE_1, SIDE_2, FAR_1, FAR_2 = range(6)
PLACES = 6
OFFSETS = np.array(
    [
        [[2, 8, 3, 0, 51, 1], [-2, -8, -1, -7, -51, 64], [4, 6, 5, 7, 38, 25], [-4, -6, -3, -5, -38, -25]],
        [[2, 8, 1, 7, 51, 64], [-2, -8, -3, 0, -51, -1], [4, 6, 3, 5, 38, 25], [-4, -6, -5, -7, -38, -25]],
    ]
)
VMEM = pl.BlockSpec(memory_space=pltpu.VMEM)
SMEM = pl.BlockSpec(memory_space=pltpu.SMEM)
HBM = pl.BlockSpec(memory_space=pltpu.MemorySpace.HBM)


def split(x):
    high = x.astype(jnp.bfloat16)
    return high, (x - high.astype(jnp.float32)).astype(jnp.bfloat16)


def dot3(a, b, dims):
    def one(x, y):
        return lax.dot_general(x, y, (dims, ((), ())), preferred_element_type=jnp.float32)

    return one(a[0], b[0]) + (one(a[0], b[1]) + one(a[1], b[0]))


def pick_kernel(rows, ids, columns, counts, omega, slots, old, sems):
    owner, member = ids[0], ids[1]
    count = counts[0]
    parity = lax.rem(owner, 2)
    choices = np.mod(OFFSETS, rows).reshape(2, -1)
    total = choices.shape[1]
    slot_count = columns.shape[1]
    wanted = [jnp.where(parity == 0, int(choices[0, i]), int(choices[1, i])) for i in range(total)]
    for i in range(total):
        slots[i] = -1

    def match(s, carry):
        offset = lax.rem(columns[0, s] - owner + rows, rows)
        for i in range(total):

            @pl.when(wanted[i] == offset)
            def _():
                slots[i] = s

        return carry

    lax.fori_loop(0, jnp.minimum(count, slot_count), match, 0)
    for k in range(PLACES):
        slot = slots[member * PLACES + k]

        @pl.when(slot >= 0)
        def _():
            pltpu.make_async_copy(omega.at[slot], old.at[k], sems.at[k]).start()

        @pl.when(slot < 0)
        def _():
            old[k] = jnp.zeros(old.shape[1:], jnp.float32)

    for k in range(PLACES):
        slot = slots[member * PLACES + k]

        @pl.when(slot >= 0)
        def _():
            pltpu.make_async_copy(omega.at[slot], old.at[k], sems.at[k]).wait()


def partial_kernel(own_side, old, full, *refs):
    column, out = refs[:PLACES], refs[PLACES]
    total = jnp.zeros(out.shape, jnp.float32)
    for k in range(PLACES):
        x = column[k][...]
        if k == SIDE_2:
            x = jnp.where(own_side[0] == 1, full[...], x)
        total = total + dot3(split(x), split(old[k]), ((1,), (1,)))
    out[...] = total


def tile_kernel(own_side, ids, half, other, full, *refs):
    column = refs[:PLACES]
    near_1, near_2, side, far_1, far_2, y_out = refs[PLACES:]
    product = half[...] + other[...]
    samples_here = y_out.shape[0]
    turned = split(product.T)
    for k in range(PLACES):
        x = column[k][...]
        if k == SIDE_2:
            x = jnp.where(own_side[0] == 1, full[...], x)
        tile = dot3(turned, split(x), ((1,), (0,)))
        if k in (SIDE_1, SIDE_2):
            side[k - SIDE_1] = tile
        else:
            {NEAR_1: near_1, NEAR_2: near_2, FAR_1: far_1, FAR_2: far_2}[k][...] = tile
    start = pl.multiple_of(ids[1] * samples_here, samples_here)
    y_out[...] = half[pl.ds(start, samples_here), :] + other[pl.ds(start, samples_here), :]


def update(before, ours, theirs, samples, corner=None):
    grad = (ours + theirs.T) / (2.0 * samples)
    if corner is not None:
        grad = grad - jnp.where(corner, 1.0 / jnp.where(corner, before, 1.0), 0.0)
    moved = before - step_size * grad
    size = jnp.maximum(jnp.abs(moved) - step_size * penalty, 0.0)
    shrunk = jnp.where(moved < 0.0, -size, size)
    return shrunk if corner is None else jnp.where(corner, moved, shrunk)


def update_far_kernel(samples, old, far_1, far_2, got_1, got_2, out):
    out[0] = update(old[FAR_1], far_1[...], got_1[...], samples)
    out[1] = update(old[FAR_2], far_2[...], got_2[...], samples)


def update_near_kernel(samples, own_side, old, near_1, near_2, side, got_1, got_2, out):
    on_self = own_side[0] == 1
    shape = out.shape[1:]
    unit = lax.broadcasted_iota(jnp.int32, shape, 0) == lax.broadcasted_iota(jnp.int32, shape, 1)
    out[NEAR_1] = update(old[NEAR_1], near_1[...], got_1[0], samples)
    out[NEAR_2] = update(old[NEAR_2], near_2[...], got_2[0], samples)
    out[SIDE_1] = update(old[SIDE_1], side[0], got_1[1], samples)
    theirs = jnp.where(on_self, side[1], got_2[1])
    out[SIDE_2] = update(old[SIDE_2], side[1], theirs, samples, jnp.logical_and(unit, on_self))


NEAR_PLACES = (NEAR_1, NEAR_2, SIDE_1, SIDE_2)
FAR_PLACES = (FAR_1, FAR_2)


def place_kernel(groups, places, fill, slots, ids, counts, *refs):
    n = len(groups)
    if fill:
        out, zero, sems, zero_sems = refs[n:]
    else:
        out, sems = refs[n + 1 :]
    found = []
    for g, j in enumerate(groups):
        for i, k in enumerate(places):
            slot = slots[lax.bitwise_xor(ids[1], j) * PLACES + k]
            copy = pltpu.make_async_copy(
                refs[g].at[i], out.at[jnp.maximum(slot, 0)], sems.at[g * len(places) + i]
            )
            found.append((slot >= 0, copy))
    for condition, copy in found:
        pl.when(condition)(copy.start)
    if fill:
        zero[...] = jnp.zeros(zero.shape, jnp.float32)
        slot_count = out.shape[0]
        first = jnp.clip(counts[0], 0, slot_count)

        @pl.loop(first, slot_count)
        def _(s):
            pltpu.make_async_copy(zero, out.at[s], zero_sems.at[s]).start()

        @pl.loop(first, slot_count)
        def _(s):
            pltpu.make_async_copy(zero, out.at[s], zero_sems.at[s]).wait()

    for condition, copy in found:
        pl.when(condition)(copy.wait)


PARAMS = pltpu.CompilerParams(vmem_limit_bytes=8 * 2**20)


def cost(flops, nbytes):
    return pl.CostEstimate(flops=flops, bytes_accessed=nbytes, transcendentals=0)


def step(omega, dosage, columns, counts):
    weights = omega[0]
    own_dosage = dosage[0]
    slot_count, block_size = weights.shape[:2]
    samples_here = own_dosage.shape[0]
    owner = lax.axis_index("blk")
    member = lax.axis_index("team")
    rows = lax.axis_size("blk")
    team = lax.axis_size("team")
    samples = samples_here * team
    f32 = jnp.float32

    def permute(x, target):
        pairs = []
        for b in range(rows):
            for t in range(team):
                b2, t2 = target(b, t)
                pairs.append((b * team + t, (b2 % rows) * team + t2))
        return lax.ppermute(x, AXES, pairs)

    def partner(b, t, k):
        there = b + OFFSETS[b % 2, t, k]
        found = [
            u for u in range(team) if (OFFSETS[there % 2, u, k] + OFFSETS[b % 2, t, k]) % rows == 0
        ]
        return there, found[0]

    def fetch(x, k):
        source = {}
        for b in range(rows):
            for t in range(team):
                b2, t2 = partner(b, t, k)
                source[b2 % rows, t2] = (b, t)
        return permute(x, lambda b, t: source[b, t])

    def beside(b, t):
        return b ^ 1, t

    ids = jnp.stack([owner, member]).astype(jnp.int32)
    own_side = jnp.logical_or(
        jnp.logical_and(owner % 2 == 0, member == 0), jnp.logical_and(owner % 2 == 1, member == 1)
    ).astype(jnp.int32)[None]
    tile_shape = jax.ShapeDtypeStruct((block_size, block_size), f32)
    tiles_shape = jax.ShapeDtypeStruct((PLACES, block_size, block_size), f32)
    tile_bytes = block_size * block_size * 4

    slots, old = pl.pallas_call(
        functools.partial(pick_kernel, rows),
        name="pick",
        out_shape=(jax.ShapeDtypeStruct((team * PLACES,), jnp.int32), tiles_shape),
        in_specs=[SMEM, SMEM, SMEM, HBM],
        out_specs=(SMEM, VMEM),
        scratch_shapes=[pltpu.SemaphoreType.DMA((PLACES,))],
        compiler_params=PARAMS,
        cost_estimate=cost(0, 2 * PLACES * tile_bytes),
    )(ids, columns, counts, pltpu.with_memory_space_constraint(weights, pltpu.MemorySpace.HBM))

    full = lax.all_gather(own_dosage, "team", axis=0, tiled=True)
    column = [None] * PLACES
    column[FAR_2] = fetch(full, FAR_2)
    column[NEAR_2] = fetch(full, NEAR_2)
    column[NEAR_1] = fetch(full, NEAR_1)
    column[FAR_1] = fetch(full, FAR_1)
    column[SIDE_2] = permute(column[NEAR_2], beside)
    column[SIDE_1] = permute(column[NEAR_1], beside)

    partial = pl.pallas_call(
        partial_kernel,
        name="partial",
        out_shape=jax.ShapeDtypeStruct((samples, block_size), f32),
        in_specs=[SMEM] + [VMEM] * (2 + PLACES),
        out_specs=VMEM,
        compiler_params=PARAMS,
        cost_estimate=cost(2 * PLACES * samples * block_size**2, 14 * samples * block_size * 4),
    )(own_side, old, full, *column)
    half = partial + permute(partial, lambda b, t: (b, t ^ 1))
    other = permute(half, lambda b, t: (b, t ^ 2))

    near_1, near_2, side, far_1, far_2, y_product = pl.pallas_call(
        tile_kernel,
        name="tiles",
        out_shape=(
            tile_shape,
            tile_shape,
            jax.ShapeDtypeStruct((2, block_size, block_size), f32),
            tile_shape,
            tile_shape,
            jax.ShapeDtypeStruct((samples_here, block_size), f32),
        ),
        in_specs=[SMEM, SMEM] + [VMEM] * (3 + PLACES),
        out_specs=(VMEM,) * 6,
        compiler_params=PARAMS,
        cost_estimate=cost(2 * PLACES * samples * block_size**2, 14 * samples * block_size * 4),
    )(own_side, ids, half, other, full, *column)

    handed = permute(side, beside)

    def back(x, k):
        return permute(x, lambda b, t: partner(b, t, k))

    got_far_2 = back(far_2, FAR_2)
    got_far_1 = back(far_1, FAR_1)
    got_2 = back(jnp.stack([near_2, handed[1]]), NEAR_2)
    got_1 = back(jnp.stack([near_1, handed[0]]), NEAR_1)

    def kernel(function, out_shape, in_specs, nbytes):
        return pl.pallas_call(
            function,
            out_shape=out_shape,
            in_specs=in_specs,
            out_specs=VMEM,
            compiler_params=PARAMS,
            cost_estimate=cost(0, nbytes),
        )

    def tiles_of(count):
        return jax.ShapeDtypeStruct((count, block_size, block_size), f32)

    far_tiles = kernel(
        functools.partial(update_far_kernel, samples), tiles_of(2), [VMEM] * 5, 8 * tile_bytes
    )(old, far_1, far_2, got_far_1, got_far_2)
    near_tiles = kernel(
        functools.partial(update_near_kernel, samples), tiles_of(4), [SMEM] + [VMEM] * 6, 16 * tile_bytes
    )(own_side, old, near_1, near_2, side, got_1, got_2)

    def chip(b, t):
        return b, t ^ 2

    def core(b, t):
        return b, t ^ 1

    far_across = permute(far_tiles, chip)
    far_mate = permute(far_tiles, core)
    near_across = permute(near_tiles, chip)
    near_mate = permute(near_tiles, core)
    far_last = permute(far_across, core)
    near_last = permute(near_across, core)

    def place(groups, places, tiles, into):
        fill = into is None
        n = len(groups)
        sems = [pltpu.SemaphoreType.DMA((n * len(places),))]
        if fill:
            scratch = [pltpu.VMEM((block_size, block_size), f32)] + sems + [pltpu.SemaphoreType.DMA((slot_count,))]
        else:
            scratch = sems
        return pl.pallas_call(
            functools.partial(place_kernel, groups, places, fill),
            out_shape=tiles_of(slot_count),
            in_specs=[SMEM] * 3 + [VMEM] * n + ([] if fill else [HBM]),
            out_specs=HBM,
            input_output_aliases={} if fill else {3 + n: 0},
            scratch_shapes=scratch,
            compiler_params=PARAMS,
            cost_estimate=cost(0, 2 * n * len(places) * tile_bytes),
        )(slots, ids, counts, *tiles, *([] if fill else [into]))

    new_omega = place((0, 1, 2, 3), FAR_PLACES, (far_tiles, far_mate, far_across, far_last), None)
    new_omega = place((0, 1, 2), NEAR_PLACES, (near_tiles, near_mate, near_across), new_omega)
    new_omega = place((3,), NEAR_PLACES, (near_last,), new_omega)
    return (new_omega[None], y_product[None])


def solution(mesh):
    return jax.shard_map(
        step,
        mesh=mesh,
        in_specs=(P("blk", None, None, None), P("blk", "team", None), P("blk", None), P("blk")),
        out_specs=(P("blk", None, None, None), P("blk", "team", None)),
        check_vma=False,
    )
```

```python
import functools

import jax
import jax.numpy as jnp
import numpy as np
from jax import lax
from jax.experimental import pallas as pl
from jax.experimental.pallas import tpu as pltpu
from jax.sharding import PartitionSpec as P


step_size = 0.1
penalty = 0.05


AXES = ("blk", "team")
NEAR_1, NEAR_2, SIDE_1, SIDE_2, FAR_1, FAR_2 = range(6)
PLACES = 6
OFFSETS = np.array(
    [
        [[4, 2, 5, 3, 51, 38], [-4, -2, -3, -1, -51, -38], [8, 6, 0, 7, 1, 25], [-8, -6, -7, -5, 64, -25]],
        [[4, 2, 3, 1, 51, 38], [-4, -2, -5, -3, -51, -38], [8, 6, 7, 5, 64, 25], [-8, -6, 0, -7, -1, -25]],
    ]
)
SELF = int(np.argwhere(OFFSETS == 0)[0, 2])
VMEM = pl.BlockSpec(memory_space=pltpu.VMEM)
SMEM = pl.BlockSpec(memory_space=pltpu.SMEM)
HBM = pl.BlockSpec(memory_space=pltpu.MemorySpace.HBM)


def split(x):
    high = x.astype(jnp.bfloat16)
    return high, (x - high.astype(jnp.float32)).astype(jnp.bfloat16)


def dot3(a, b, dims):
    def one(x, y):
        return lax.dot_general(x, y, (dims, ((), ())), preferred_element_type=jnp.float32)

    return one(a[0], b[0]) + (one(a[0], b[1]) + one(a[1], b[0]))


def pick_kernel(rows, ids, columns, counts, omega, slots, old, sems):
    owner, member = ids[0], ids[1]
    count = counts[0]
    parity = lax.rem(owner, 2)
    choices = np.mod(OFFSETS, rows).reshape(2, -1)
    total = choices.shape[1]
    slot_count = columns.shape[1]
    wanted = [jnp.where(parity == 0, int(choices[0, i]), int(choices[1, i])) for i in range(total)]
    for i in range(total):
        slots[i] = -1

    def match(s, carry):
        offset = lax.rem(columns[0, s] - owner + rows, rows)
        for i in range(total):

            @pl.when(wanted[i] == offset)
            def _():
                slots[i] = s

        return carry

    lax.fori_loop(0, jnp.minimum(count, slot_count), match, 0)
    for k in range(PLACES):
        slot = slots[member * PLACES + k]

        @pl.when(slot >= 0)
        def _():
            pltpu.make_async_copy(omega.at[slot], old.at[k], sems.at[k]).start()

        @pl.when(slot < 0)
        def _():
            old[k] = jnp.zeros(old.shape[1:], jnp.float32)

    for k in range(PLACES):
        slot = slots[member * PLACES + k]

        @pl.when(slot >= 0)
        def _():
            pltpu.make_async_copy(omega.at[slot], old.at[k], sems.at[k]).wait()


def partial_kernel(own_side, old, full, *refs):
    column, out = refs[:PLACES], refs[PLACES]
    total = jnp.zeros(out.shape, jnp.float32)
    for k in range(PLACES):
        x = column[k][...]
        if k == SELF:
            x = jnp.where(own_side[0] == 1, full[...], x)
        total = total + dot3(split(x), split(old[k]), ((1,), (1,)))
    out[...] = total


def tile_kernel(own_side, ids, half, other, full, *refs):
    column = refs[:PLACES]
    near_1, near_2, side, far_1, far_2, y_out = refs[PLACES:]
    product = half[...] + other[...]
    samples_here = y_out.shape[0]
    turned = split(product.T)
    for k in range(PLACES):
        x = column[k][...]
        if k == SELF:
            x = jnp.where(own_side[0] == 1, full[...], x)
        tile = dot3(turned, split(x), ((1,), (0,)))
        if k in (SIDE_1, SIDE_2):
            side[k - SIDE_1] = tile
        else:
            {NEAR_1: near_1, NEAR_2: near_2, FAR_1: far_1, FAR_2: far_2}[k][...] = tile
    start = pl.multiple_of(ids[1] * samples_here, samples_here)
    y_out[...] = half[pl.ds(start, samples_here), :] + other[pl.ds(start, samples_here), :]


def update(before, ours, theirs, samples, corner=None):
    grad = (ours + theirs.T) / (2.0 * samples)
    if corner is not None:
        grad = grad - jnp.where(corner, 1.0 / jnp.where(corner, before, 1.0), 0.0)
    moved = before - step_size * grad
    size = jnp.maximum(jnp.abs(moved) - step_size * penalty, 0.0)
    shrunk = jnp.where(moved < 0.0, -size, size)
    return shrunk if corner is None else jnp.where(corner, moved, shrunk)


def update_far_kernel(samples, old, far_1, far_2, got_1, got_2, out):
    out[0] = update(old[FAR_1], far_1[...], got_1[...], samples)
    out[1] = update(old[FAR_2], far_2[...], got_2[...], samples)


def update_near_kernel(samples, own_side, old, near_1, near_2, side, got_1, got_2, out):
    on_self = own_side[0] == 1
    shape = out.shape[1:]
    unit = lax.broadcasted_iota(jnp.int32, shape, 0) == lax.broadcasted_iota(jnp.int32, shape, 1)
    corner = jnp.logical_and(unit, on_self)
    ours = [near_1[...], near_2[...], side[0], side[1]]
    theirs = [got_1[0], got_2[0], got_1[1], got_2[1]]
    for k in NEAR_PLACES:
        if k == SELF:
            given = jnp.where(on_self, ours[k], theirs[k])
            out[k] = update(old[k], ours[k], given, samples, corner)
        else:
            out[k] = update(old[k], ours[k], theirs[k], samples)


NEAR_PLACES = (NEAR_1, NEAR_2, SIDE_1, SIDE_2)
FAR_PLACES = (FAR_1, FAR_2)


def blank_kernel(counts, out, zero, sems):
    zero[...] = jnp.zeros(zero.shape, jnp.float32)
    slot_count = out.shape[0]
    first = jnp.clip(counts[0], 0, slot_count)

    @pl.loop(first, slot_count)
    def _(s):
        pltpu.make_async_copy(zero, out.at[s], sems.at[s]).start()

    @pl.loop(first, slot_count)
    def _(s):
        pltpu.make_async_copy(zero, out.at[s], sems.at[s]).wait()


def place_kernel(groups, places, slots, ids, *refs):
    out, sems = refs[len(groups) + 1 :]
    found = []
    for g, j in enumerate(groups):
        for i, k in enumerate(places):
            slot = slots[lax.bitwise_xor(ids[1], j) * PLACES + k]
            copy = pltpu.make_async_copy(
                refs[g].at[i], out.at[jnp.maximum(slot, 0)], sems.at[g * len(places) + i]
            )
            found.append((slot >= 0, copy))
    for condition, copy in found:
        pl.when(condition)(copy.start)
    for condition, copy in found:
        pl.when(condition)(copy.wait)


PARAMS = pltpu.CompilerParams(vmem_limit_bytes=8 * 2**20)


def cost(flops, nbytes):
    return pl.CostEstimate(flops=flops, bytes_accessed=nbytes, transcendentals=0)


def step(omega, dosage, columns, counts):
    weights = omega[0]
    own_dosage = dosage[0]
    slot_count, block_size = weights.shape[:2]
    samples_here = own_dosage.shape[0]
    owner = lax.axis_index("blk")
    member = lax.axis_index("team")
    rows = lax.axis_size("blk")
    team = lax.axis_size("team")
    samples = samples_here * team
    f32 = jnp.float32

    def permute(x, target):
        pairs = []
        for b in range(rows):
            for t in range(team):
                b2, t2 = target(b, t)
                pairs.append((b * team + t, (b2 % rows) * team + t2))
        return lax.ppermute(x, AXES, pairs)

    def partner(b, t, k):
        there = b + OFFSETS[b % 2, t, k]
        found = [
            u for u in range(team) if (OFFSETS[there % 2, u, k] + OFFSETS[b % 2, t, k]) % rows == 0
        ]
        return there, found[0]

    def fetch(x, k):
        source = {}
        for b in range(rows):
            for t in range(team):
                b2, t2 = partner(b, t, k)
                source[b2 % rows, t2] = (b, t)
        return permute(x, lambda b, t: source[b, t])

    def beside(b, t):
        return b ^ 1, t

    ids = jnp.stack([owner, member]).astype(jnp.int32)
    own_side = jnp.logical_or(
        jnp.logical_and(owner % 2 == 0, member == 2), jnp.logical_and(owner % 2 == 1, member == 3)
    ).astype(jnp.int32)[None]
    tile_shape = jax.ShapeDtypeStruct((block_size, block_size), f32)
    tiles_shape = jax.ShapeDtypeStruct((PLACES, block_size, block_size), f32)
    tile_bytes = block_size * block_size * 4

    slots, old = pl.pallas_call(
        functools.partial(pick_kernel, rows),
        name="pick",
        out_shape=(jax.ShapeDtypeStruct((team * PLACES,), jnp.int32), tiles_shape),
        in_specs=[SMEM, SMEM, SMEM, HBM],
        out_specs=(SMEM, VMEM),
        scratch_shapes=[pltpu.SemaphoreType.DMA((PLACES,))],
        compiler_params=PARAMS,
        cost_estimate=cost(0, 2 * PLACES * tile_bytes),
    )(ids, columns, counts, pltpu.with_memory_space_constraint(weights, pltpu.MemorySpace.HBM))

    full = lax.all_gather(own_dosage, "team", axis=0, tiled=True)
    column = [None] * PLACES
    column[FAR_2] = fetch(full, FAR_2)
    column[NEAR_2] = fetch(full, NEAR_2)
    column[NEAR_1] = fetch(full, NEAR_1)
    column[FAR_1] = fetch(full, FAR_1)
    column[SIDE_2] = permute(column[NEAR_2], beside)
    column[SIDE_1] = permute(column[NEAR_1], beside)

    partial = pl.pallas_call(
        partial_kernel,
        name="partial",
        out_shape=jax.ShapeDtypeStruct((samples, block_size), f32),
        in_specs=[SMEM] + [VMEM] * (2 + PLACES),
        out_specs=VMEM,
        compiler_params=PARAMS,
        cost_estimate=cost(2 * PLACES * samples * block_size**2, 14 * samples * block_size * 4),
    )(own_side, old, full, *column)
    half = partial + permute(partial, lambda b, t: (b, t ^ 1))
    other = permute(half, lambda b, t: (b, t ^ 2))

    near_1, near_2, side, far_1, far_2, y_product = pl.pallas_call(
        tile_kernel,
        name="tiles",
        out_shape=(
            tile_shape,
            tile_shape,
            jax.ShapeDtypeStruct((2, block_size, block_size), f32),
            tile_shape,
            tile_shape,
            jax.ShapeDtypeStruct((samples_here, block_size), f32),
        ),
        in_specs=[SMEM, SMEM] + [VMEM] * (3 + PLACES),
        out_specs=(VMEM,) * 6,
        compiler_params=PARAMS,
        cost_estimate=cost(2 * PLACES * samples * block_size**2, 14 * samples * block_size * 4),
    )(own_side, ids, half, other, full, *column)

    handed = permute(side, beside)

    def back(x, k):
        return permute(x, lambda b, t: partner(b, t, k))

    got_far_2 = back(far_2, FAR_2)
    got_far_1 = back(far_1, FAR_1)
    got_2 = back(jnp.stack([near_2, handed[1]]), NEAR_2)
    got_1 = back(jnp.stack([near_1, handed[0]]), NEAR_1)

    def kernel(function, out_shape, in_specs, nbytes):
        return pl.pallas_call(
            function,
            out_shape=out_shape,
            in_specs=in_specs,
            out_specs=VMEM,
            compiler_params=PARAMS,
            cost_estimate=cost(0, nbytes),
        )

    def tiles_of(count):
        return jax.ShapeDtypeStruct((count, block_size, block_size), f32)

    far_tiles = kernel(
        functools.partial(update_far_kernel, samples), tiles_of(2), [VMEM] * 5, 8 * tile_bytes
    )(old, far_1, far_2, got_far_1, got_far_2)
    near_tiles = kernel(
        functools.partial(update_near_kernel, samples), tiles_of(4), [SMEM] + [VMEM] * 6, 16 * tile_bytes
    )(own_side, old, near_1, near_2, side, got_1, got_2)

    def chip(b, t):
        return b, t ^ 2

    def core(b, t):
        return b, t ^ 1

    far_across = permute(far_tiles, chip)
    far_mate = permute(far_tiles, core)
    near_across = permute(near_tiles, chip)
    near_mate = permute(near_tiles, core)
    far_last = permute(far_across, core)
    near_last = permute(near_across, core)

    new_omega = pl.pallas_call(
        blank_kernel,
        name="blank",
        out_shape=tiles_of(slot_count),
        in_specs=[SMEM],
        out_specs=HBM,
        scratch_shapes=[
            pltpu.VMEM((block_size, block_size), f32),
            pltpu.SemaphoreType.DMA((slot_count,)),
        ],
        compiler_params=PARAMS,
        cost_estimate=cost(0, PLACES * tile_bytes),
    )(counts)

    def place(groups, places, tiles, into):
        n = len(groups)
        return pl.pallas_call(
            functools.partial(place_kernel, groups, places),
            out_shape=tiles_of(slot_count),
            in_specs=[SMEM] * 2 + [VMEM] * n + [HBM],
            out_specs=HBM,
            input_output_aliases={2 + n: 0},
            scratch_shapes=[pltpu.SemaphoreType.DMA((n * len(places),))],
            compiler_params=PARAMS,
            cost_estimate=cost(0, 2 * n * len(places) * tile_bytes),
        )(slots, ids, *tiles, into)

    new_omega = place((0, 1, 2, 3), FAR_PLACES, (far_tiles, far_mate, far_across, far_last), new_omega)
    new_omega = place((0, 1, 2), NEAR_PLACES, (near_tiles, near_mate, near_across), new_omega)
    new_omega = place((3,), NEAR_PLACES, (near_last,), new_omega)
    return (new_omega[None], y_product[None])


def solution(mesh):
    return jax.shard_map(
        step,
        mesh=mesh,
        in_specs=(P("blk", None, None, None), P("blk", "team", None), P("blk", None), P("blk")),
        out_specs=(P("blk", None, None, None), P("blk", "team", None)),
        check_vma=False,
    )
```

```python
import functools

import jax
import jax.numpy as jnp
import numpy as np
from jax import lax
from jax.experimental import pallas as pl
from jax.experimental.pallas import tpu as pltpu
from jax.sharding import PartitionSpec as P


step_size = 0.1
penalty = 0.05


AXES = ("blk", "team")
NEAR_1, NEAR_2, SIDE_1, SIDE_2, FAR_1, FAR_2 = range(6)
PLACES = 6
NEAR = ((4, 2), (8, 6))
FAR = ((51, 38), (0, 25))


def offsets(near, far):
    table = np.zeros((2, 4, PLACES), int)
    for parity in range(2):
        for t in range(4):
            sign = 1 - 2 * (t % 2)
            for i in range(2):
                near_by = sign * near[t // 2][i]
                side = near_by + 1 - 2 * parity
                distant = sign * far[t // 2][i]
                if distant == 0:
                    distant = 1 - 2 * parity if parity == t % 2 else 64
                table[parity, t, i] = near_by
                table[parity, t, 2 + i] = 0 if abs(side) == 9 else side
                table[parity, t, 4 + i] = distant
    return table


OFFSETS = offsets(NEAR, FAR)
VMEM = pl.BlockSpec(memory_space=pltpu.VMEM)
SMEM = pl.BlockSpec(memory_space=pltpu.SMEM)
HBM = pl.BlockSpec(memory_space=pltpu.MemorySpace.HBM)


def split(x):
    high = x.astype(jnp.bfloat16)
    return high, (x - high.astype(jnp.float32)).astype(jnp.bfloat16)


def dot3(a, b, dims):
    def one(x, y):
        return lax.dot_general(x, y, (dims, ((), ())), preferred_element_type=jnp.float32)

    return one(a[0], b[0]) + (one(a[0], b[1]) + one(a[1], b[0]))


def pick_kernel(rows, offset_table, ids, columns, counts, omega, slots, old, sems):
    owner, member = ids[0], ids[1]
    count = counts[0]
    parity = lax.rem(owner, 2)
    choices = np.mod(np.array(offset_table), rows).reshape(2, -1)
    total = choices.shape[1]
    slot_count = columns.shape[1]
    wanted = [jnp.where(parity == 0, int(choices[0, i]), int(choices[1, i])) for i in range(total)]
    for i in range(total):
        slots[i] = -1

    def match(s, carry):
        offset = lax.rem(columns[0, s] - owner + rows, rows)
        for i in range(total):

            @pl.when(wanted[i] == offset)
            def _():
                slots[i] = s

        return carry

    lax.fori_loop(0, jnp.minimum(count, slot_count), match, 0)
    for k in range(PLACES):
        slot = slots[member * PLACES + k]

        @pl.when(slot >= 0)
        def _():
            pltpu.make_async_copy(omega.at[slot], old.at[k], sems.at[k]).start()

        @pl.when(slot < 0)
        def _():
            old[k] = jnp.zeros(old.shape[1:], jnp.float32)

    for k in range(PLACES):
        slot = slots[member * PLACES + k]

        @pl.when(slot >= 0)
        def _():
            pltpu.make_async_copy(omega.at[slot], old.at[k], sems.at[k]).wait()


def partial_kernel(self_place, own_side, old, full, *refs):
    column, out = refs[:PLACES], refs[PLACES]
    total = jnp.zeros(out.shape, jnp.float32)
    for k in range(PLACES):
        x = column[k][...]
        if k == self_place:
            x = jnp.where(own_side[0] == 1, full[...], x)
        total = total + dot3(split(x), split(old[k]), ((1,), (1,)))
    out[...] = total


def turn_kernel(self_place, own_side, full, *refs):
    column, (high, low) = refs[:PLACES], refs[PLACES:]
    block_size = full.shape[1]
    for k in range(PLACES):
        x = column[k][...]
        if k == self_place:
            x = jnp.where(own_side[0] == 1, full[...], x)
        here = pl.ds(k * block_size, block_size)
        high[here, :], low[here, :] = split(x.T)


def tile_kernel(ids, half, other, high, low, *outs):
    near_1, near_2, side, far_1, far_2, y_out = outs
    samples_here, block_size = y_out.shape
    product_high, product_low = split(half[...] + other[...])

    def one(x, y):
        return jnp.dot(x, y, preferred_element_type=jnp.float32)

    both = one(high[...], jnp.concatenate([product_high, product_low], axis=1))
    rest = one(low[...], product_high)
    tiles = both[:, :block_size] + (both[:, block_size:] + rest)
    for k in range(PLACES):
        tile = tiles[k * block_size : (k + 1) * block_size]
        if k in (SIDE_1, SIDE_2):
            side[k - SIDE_1] = tile
        else:
            {NEAR_1: near_1, NEAR_2: near_2, FAR_1: far_1, FAR_2: far_2}[k][...] = tile
    start = pl.multiple_of(ids[1] * samples_here, samples_here)
    y_out[...] = half[pl.ds(start, samples_here), :] + other[pl.ds(start, samples_here), :]


def update(before, ours, theirs, samples, corner=None):
    grad = (ours.T + theirs) / (2.0 * samples)
    if corner is not None:
        grad = grad - jnp.where(corner, 1.0 / jnp.where(corner, before, 1.0), 0.0)
    moved = before - step_size * grad
    size = jnp.maximum(jnp.abs(moved) - step_size * penalty, 0.0)
    shrunk = jnp.where(moved < 0.0, -size, size)
    return shrunk if corner is None else jnp.where(corner, moved, shrunk)


def update_far_kernel(samples, old, far_1, far_2, got_1, got_2, out):
    out[0] = update(old[FAR_1], far_1[...], got_1[...], samples)
    out[1] = update(old[FAR_2], far_2[...], got_2[...], samples)


def update_near_kernel(self_place, samples, own_side, old, near_1, near_2, side, got_1, got_2, out):
    on_self = own_side[0] == 1
    shape = out.shape[1:]
    unit = lax.broadcasted_iota(jnp.int32, shape, 0) == lax.broadcasted_iota(jnp.int32, shape, 1)
    corner = jnp.logical_and(unit, on_self)
    ours = [near_1[...], near_2[...], side[0], side[1]]
    theirs = [got_1[0], got_2[0], got_1[1], got_2[1]]
    for k in NEAR_PLACES:
        if k == self_place:
            given = jnp.where(on_self, ours[k], theirs[k])
            out[k] = update(old[k], ours[k], given, samples, corner)
        else:
            out[k] = update(old[k], ours[k], theirs[k], samples)


NEAR_PLACES = (NEAR_1, NEAR_2, SIDE_1, SIDE_2)
FAR_PLACES = (FAR_1, FAR_2)


def blank_kernel(counts, out, zero, sems):
    zero[...] = jnp.zeros(zero.shape, jnp.float32)
    slot_count = out.shape[0]
    first = jnp.clip(counts[0], 0, slot_count)

    @pl.loop(first, slot_count)
    def _(s):
        pltpu.make_async_copy(zero, out.at[s], sems.at[s]).start()

    @pl.loop(first, slot_count)
    def _(s):
        pltpu.make_async_copy(zero, out.at[s], sems.at[s]).wait()


def place_kernel(groups, places, slots, ids, *refs):
    out, sems = refs[len(groups) + 1 :]
    found = []
    for g, j in enumerate(groups):
        for i, k in enumerate(places):
            slot = slots[lax.bitwise_xor(ids[1], j) * PLACES + k]
            copy = pltpu.make_async_copy(
                refs[g].at[i], out.at[jnp.maximum(slot, 0)], sems.at[g * len(places) + i]
            )
            found.append((slot >= 0, copy))
    for condition, copy in found:
        pl.when(condition)(copy.start)
    for condition, copy in found:
        pl.when(condition)(copy.wait)


PARAMS = pltpu.CompilerParams(vmem_limit_bytes=8 * 2**20)


def cost(flops, nbytes):
    return pl.CostEstimate(flops=flops, bytes_accessed=nbytes, transcendentals=0)


def step(omega, dosage, columns, counts):
    weights = omega[0]
    own_dosage = dosage[0]
    slot_count, block_size = weights.shape[:2]
    samples_here = own_dosage.shape[0]
    owner = lax.axis_index("blk")
    member = lax.axis_index("team")
    rows = lax.axis_size("blk")
    team = lax.axis_size("team")
    samples = samples_here * team
    f32 = jnp.float32

    def permute(x, target):
        pairs = []
        for b in range(rows):
            for t in range(team):
                b2, t2 = target(b, t)
                pairs.append((b * team + t, (b2 % rows) * team + t2))
        return lax.ppermute(x, AXES, pairs)

    def partner(b, t, k):
        there = b + OFFSETS[b % 2, t, k]
        found = [
            u for u in range(team) if (OFFSETS[there % 2, u, k] + OFFSETS[b % 2, t, k]) % rows == 0
        ]
        return there, found[0]

    def fetch(x, k):
        source = {}
        for b in range(rows):
            for t in range(team):
                b2, t2 = partner(b, t, k)
                source[b2 % rows, t2] = (b, t)
        return permute(x, lambda b, t: source[b, t])

    def beside(b, t):
        return b ^ 1, t

    ids = jnp.stack([owner, member]).astype(jnp.int32)
    table = tuple(tuple(map(tuple, half.tolist())) for half in OFFSETS)
    self_even, self_odd = np.argwhere(OFFSETS == 0).tolist()
    self_place = self_even[2]
    own_side = (member == jnp.where(owner % 2 == 0, self_even[1], self_odd[1])).astype(jnp.int32)[None]
    tile_shape = jax.ShapeDtypeStruct((block_size, block_size), f32)
    tiles_shape = jax.ShapeDtypeStruct((PLACES, block_size, block_size), f32)
    tile_bytes = block_size * block_size * 4

    slots, old = pl.pallas_call(
        functools.partial(pick_kernel, rows, table),
        name="pick",
        out_shape=(jax.ShapeDtypeStruct((team * PLACES,), jnp.int32), tiles_shape),
        in_specs=[SMEM, SMEM, SMEM, HBM],
        out_specs=(SMEM, VMEM),
        scratch_shapes=[pltpu.SemaphoreType.DMA((PLACES,))],
        compiler_params=PARAMS,
        cost_estimate=cost(0, 2 * PLACES * tile_bytes),
    )(ids, columns, counts, pltpu.with_memory_space_constraint(weights, pltpu.MemorySpace.HBM))

    full = lax.all_gather(own_dosage, "team", axis=0, tiled=True)
    column = [None] * PLACES
    column[FAR_2] = fetch(full, FAR_2)
    column[NEAR_2] = fetch(full, NEAR_2)
    column[NEAR_1] = fetch(full, NEAR_1)
    column[FAR_1] = fetch(full, FAR_1)
    column[SIDE_2] = permute(column[NEAR_2], beside)
    column[SIDE_1] = permute(column[NEAR_1], beside)

    partial = pl.pallas_call(
        functools.partial(partial_kernel, self_place),
        name="partial",
        out_shape=jax.ShapeDtypeStruct((samples, block_size), f32),
        in_specs=[SMEM] + [VMEM] * (2 + PLACES),
        out_specs=VMEM,
        compiler_params=PARAMS,
        cost_estimate=cost(2 * PLACES * samples * block_size**2, 14 * samples * block_size * 4),
    )(own_side, old, full, *column)
    half = partial + permute(partial, lambda b, t: (b, t ^ 1))
    other = permute(half, lambda b, t: (b, t ^ 2))

    turned = jax.ShapeDtypeStruct((PLACES * block_size, samples), jnp.bfloat16)
    high, low = pl.pallas_call(
        functools.partial(turn_kernel, self_place),
        name="turn",
        out_shape=(turned, turned),
        in_specs=[SMEM] + [VMEM] * (1 + PLACES),
        out_specs=(VMEM, VMEM),
        compiler_params=PARAMS,
        cost_estimate=cost(0, 14 * samples * block_size * 4),
    )(own_side, full, *column)
    near_1, near_2, side, far_1, far_2, y_product = pl.pallas_call(
        tile_kernel,
        name="tiles",
        out_shape=(
            tile_shape,
            tile_shape,
            jax.ShapeDtypeStruct((2, block_size, block_size), f32),
            tile_shape,
            tile_shape,
            jax.ShapeDtypeStruct((samples_here, block_size), f32),
        ),
        in_specs=[SMEM] + [VMEM] * 4,
        out_specs=(VMEM,) * 6,
        compiler_params=PARAMS,
        cost_estimate=cost(2 * PLACES * samples * block_size**2, 14 * samples * block_size * 4),
    )(ids, half, other, high, low)

    handed = permute(side, beside)

    def back(x, k):
        return permute(x, lambda b, t: partner(b, t, k))

    got_far_2 = back(far_2, FAR_2)
    got_far_1 = back(far_1, FAR_1)
    got_2 = back(jnp.stack([near_2, handed[1]]), NEAR_2)
    got_1 = back(jnp.stack([near_1, handed[0]]), NEAR_1)

    def kernel(function, out_shape, in_specs, nbytes):
        return pl.pallas_call(
            function,
            out_shape=out_shape,
            in_specs=in_specs,
            out_specs=VMEM,
            compiler_params=PARAMS,
            cost_estimate=cost(0, nbytes),
        )

    def tiles_of(count):
        return jax.ShapeDtypeStruct((count, block_size, block_size), f32)

    far_tiles = kernel(
        functools.partial(update_far_kernel, samples), tiles_of(2), [VMEM] * 5, 8 * tile_bytes
    )(old, far_1, far_2, got_far_1, got_far_2)
    near_tiles = kernel(
        functools.partial(update_near_kernel, self_place, samples), tiles_of(4), [SMEM] + [VMEM] * 6, 16 * tile_bytes
    )(own_side, old, near_1, near_2, side, got_1, got_2)

    def chip(b, t):
        return b, t ^ 2

    def core(b, t):
        return b, t ^ 1

    far_across = permute(far_tiles, chip)
    far_mate = permute(far_tiles, core)
    near_across = permute(near_tiles, chip)
    near_mate = permute(near_tiles, core)
    far_last = permute(far_across, core)
    near_last = permute(near_across, core)

    new_omega = pl.pallas_call(
        blank_kernel,
        name="blank",
        out_shape=tiles_of(slot_count),
        in_specs=[SMEM],
        out_specs=HBM,
        scratch_shapes=[
            pltpu.VMEM((block_size, block_size), f32),
            pltpu.SemaphoreType.DMA((slot_count,)),
        ],
        compiler_params=PARAMS,
        cost_estimate=cost(0, PLACES * tile_bytes),
    )(counts)

    def place(groups, places, tiles, into):
        n = len(groups)
        return pl.pallas_call(
            functools.partial(place_kernel, groups, places),
            out_shape=tiles_of(slot_count),
            in_specs=[SMEM] * 2 + [VMEM] * n + [HBM],
            out_specs=HBM,
            input_output_aliases={2 + n: 0},
            scratch_shapes=[pltpu.SemaphoreType.DMA((n * len(places),))],
            compiler_params=PARAMS,
            cost_estimate=cost(0, 2 * n * len(places) * tile_bytes),
        )(slots, ids, *tiles, into)

    new_omega = place((0, 1, 2, 3), FAR_PLACES, (far_tiles, far_mate, far_across, far_last), new_omega)
    new_omega = place((0, 1, 2), NEAR_PLACES, (near_tiles, near_mate, near_across), new_omega)
    new_omega = place((3,), NEAR_PLACES, (near_last,), new_omega)
    return (new_omega[None], y_product[None])


def solution(mesh):
    return jax.shard_map(
        step,
        mesh=mesh,
        in_specs=(P("blk", None, None, None), P("blk", "team", None), P("blk", None), P("blk")),
        out_specs=(P("blk", None, None, None), P("blk", "team", None)),
        check_vma=False,
    )
```

```python
import functools

import jax
import jax.numpy as jnp
import numpy as np
from jax import lax
from jax.experimental import pallas as pl
from jax.experimental.pallas import tpu as pltpu
from jax.sharding import PartitionSpec as P


step_size = 0.1
penalty = 0.05


AXES = ("blk", "team")
NEAR_1, NEAR_2, SIDE_1, SIDE_2, FAR_1, FAR_2 = range(6)
PLACES = 6
NEAR = ((4, 2), (8, 6))
FAR = ((51, 38), (0, 25))


def offsets(near, far):
    table = np.zeros((2, 4, PLACES), int)
    for parity in range(2):
        for t in range(4):
            sign = 1 - 2 * (t % 2)
            for i in range(2):
                near_by = sign * near[t // 2][i]
                side = near_by + 1 - 2 * parity
                distant = sign * far[t // 2][i]
                if distant == 0:
                    distant = 1 - 2 * parity if parity == t % 2 else 64
                table[parity, t, i] = near_by
                table[parity, t, 2 + i] = 0 if abs(side) == 9 else side
                table[parity, t, 4 + i] = distant
    return table


OFFSETS = offsets(NEAR, FAR)
VMEM = pl.BlockSpec(memory_space=pltpu.VMEM)
SMEM = pl.BlockSpec(memory_space=pltpu.SMEM)
HBM = pl.BlockSpec(memory_space=pltpu.MemorySpace.HBM)


def split(x):
    high = x.astype(jnp.bfloat16)
    return high, (x - high.astype(jnp.float32)).astype(jnp.bfloat16)


def dot3(a, b, dims):
    def one(x, y):
        return lax.dot_general(x, y, (dims, ((), ())), preferred_element_type=jnp.float32)

    return one(a[0], b[0]) + (one(a[0], b[1]) + one(a[1], b[0]))


def pick_kernel(rows, offset_table, ids, columns, counts, omega, slots, old, sems):
    owner, member = ids[0], ids[1]
    count = counts[0]
    parity = lax.rem(owner, 2)
    choices = np.mod(np.array(offset_table), rows).reshape(2, -1)
    total = choices.shape[1]
    slot_count = columns.shape[1]
    wanted = [jnp.where(parity == 0, int(choices[0, i]), int(choices[1, i])) for i in range(total)]
    for i in range(total):
        slots[i] = -1

    def match(s, carry):
        offset = lax.rem(columns[0, s] - owner + rows, rows)
        for i in range(total):

            @pl.when(wanted[i] == offset)
            def _():
                slots[i] = s

        return carry

    lax.fori_loop(0, jnp.minimum(count, slot_count), match, 0)
    for k in range(PLACES):
        slot = slots[member * PLACES + k]

        @pl.when(slot >= 0)
        def _():
            pltpu.make_async_copy(omega.at[slot], old.at[k], sems.at[k]).start()

        @pl.when(slot < 0)
        def _():
            old[k] = jnp.zeros(old.shape[1:], jnp.float32)

    for k in range(PLACES):
        slot = slots[member * PLACES + k]

        @pl.when(slot >= 0)
        def _():
            pltpu.make_async_copy(omega.at[slot], old.at[k], sems.at[k]).wait()


def partial_kernel(self_place, own_side, old, full, *refs):
    column, out = refs[:PLACES], refs[PLACES]
    total = jnp.zeros(out.shape, jnp.float32)
    for k in range(PLACES):
        x = column[k][...]
        if k == self_place:
            x = jnp.where(own_side[0] == 1, full[...], x)
        total = total + dot3(split(x), split(old[k]), ((1,), (1,)))
    out[...] = total


def turn_kernel(self_place, own_side, full, *refs):
    column, (high, low) = refs[:PLACES], refs[PLACES:]
    block_size = full.shape[1]
    for k in range(PLACES):
        x = column[k][...]
        if k == self_place:
            x = jnp.where(own_side[0] == 1, full[...], x)
        here = pl.ds(k * block_size, block_size)
        high[here, :], low[here, :] = split(x.T)


def tile_kernel(ids, half, other, high, low, *outs):
    near_1, near_2, side, far_1, far_2, y_out = outs
    samples_here, block_size = y_out.shape
    product_high, product_low = split(half[...] + other[...])

    def one(x, y):
        return jnp.dot(x, y, preferred_element_type=jnp.float32)

    both = one(high[...], jnp.concatenate([product_high, product_low], axis=1))
    rest = one(low[...], product_high)
    tiles = both[:, :block_size] + (both[:, block_size:] + rest)
    for k in range(PLACES):
        tile = tiles[k * block_size : (k + 1) * block_size]
        if k in (SIDE_1, SIDE_2):
            side[k - SIDE_1] = tile
        else:
            {NEAR_1: near_1, NEAR_2: near_2, FAR_1: far_1, FAR_2: far_2}[k][...] = tile
    start = pl.multiple_of(ids[1] * samples_here, samples_here)
    y_out[...] = half[pl.ds(start, samples_here), :] + other[pl.ds(start, samples_here), :]


def update(before, ours, theirs, samples, corner=None):
    grad = (ours.T + theirs) / (2.0 * samples)
    if corner is not None:
        grad = grad - jnp.where(corner, 1.0 / jnp.where(corner, before, 1.0), 0.0)
    moved = before - step_size * grad
    size = jnp.maximum(jnp.abs(moved) - step_size * penalty, 0.0)
    shrunk = jnp.where(moved < 0.0, -size, size)
    return shrunk if corner is None else jnp.where(corner, moved, shrunk)


def update_far_kernel(samples, old, far_1, far_2, got_1, got_2, near, far, every):
    far[0] = update(old[FAR_1], far_1[...], got_1[...], samples)
    far[1] = update(old[FAR_2], far_2[...], got_2[...], samples)
    for k in NEAR_PLACES:
        every[k] = near[k]
    for i, k in enumerate(FAR_PLACES):
        every[k] = far[i]


def update_near_kernel(self_place, samples, own_side, old, near_1, near_2, side, got_1, got_2, out):
    on_self = own_side[0] == 1
    shape = out.shape[1:]
    unit = lax.broadcasted_iota(jnp.int32, shape, 0) == lax.broadcasted_iota(jnp.int32, shape, 1)
    corner = jnp.logical_and(unit, on_self)
    ours = [near_1[...], near_2[...], side[0], side[1]]
    theirs = [got_1[0], got_2[0], got_1[1], got_2[1]]
    for k in NEAR_PLACES:
        if k == self_place:
            given = jnp.where(on_self, ours[k], theirs[k])
            out[k] = update(old[k], ours[k], given, samples, corner)
        else:
            out[k] = update(old[k], ours[k], theirs[k], samples)


NEAR_PLACES = (NEAR_1, NEAR_2, SIDE_1, SIDE_2)
FAR_PLACES = (FAR_1, FAR_2)


def blank_kernel(counts, out, zero, sems):
    zero[...] = jnp.zeros(zero.shape, jnp.float32)
    slot_count = out.shape[0]
    first = jnp.clip(counts[0], 0, slot_count)

    @pl.loop(first, slot_count)
    def _(s):
        pltpu.make_async_copy(zero, out.at[s], sems.at[s]).start()

    @pl.loop(first, slot_count)
    def _(s):
        pltpu.make_async_copy(zero, out.at[s], sems.at[s]).wait()


def place_kernel(groups, slots, ids, *refs):
    out, sems = refs[len(groups) + 1 :]
    found = []
    for (j, places), tiles in zip(groups, refs):
        for i, k in enumerate(places):
            slot = slots[lax.bitwise_xor(ids[1], j) * PLACES + k]
            copy = pltpu.make_async_copy(
                tiles.at[i], out.at[jnp.maximum(slot, 0)], sems.at[len(found)]
            )
            found.append((slot >= 0, copy))
    for condition, copy in found:
        pl.when(condition)(copy.start)
    for condition, copy in found:
        pl.when(condition)(copy.wait)


PARAMS = pltpu.CompilerParams(vmem_limit_bytes=8 * 2**20)


def cost(flops, nbytes):
    return pl.CostEstimate(flops=flops, bytes_accessed=nbytes, transcendentals=0)


def step(omega, dosage, columns, counts):
    weights = omega[0]
    own_dosage = dosage[0]
    slot_count, block_size = weights.shape[:2]
    samples_here = own_dosage.shape[0]
    owner = lax.axis_index("blk")
    member = lax.axis_index("team")
    rows = lax.axis_size("blk")
    team = lax.axis_size("team")
    samples = samples_here * team
    f32 = jnp.float32

    def permute(x, target):
        pairs = []
        for b in range(rows):
            for t in range(team):
                b2, t2 = target(b, t)
                pairs.append((b * team + t, (b2 % rows) * team + t2))
        return lax.ppermute(x, AXES, pairs)

    def partner(b, t, k):
        there = b + OFFSETS[b % 2, t, k]
        found = [
            u for u in range(team) if (OFFSETS[there % 2, u, k] + OFFSETS[b % 2, t, k]) % rows == 0
        ]
        return there, found[0]

    def fetch(x, k):
        source = {}
        for b in range(rows):
            for t in range(team):
                b2, t2 = partner(b, t, k)
                source[b2 % rows, t2] = (b, t)
        return permute(x, lambda b, t: source[b, t])

    def beside(b, t):
        return b ^ 1, t

    ids = jnp.stack([owner, member]).astype(jnp.int32)
    table = tuple(tuple(map(tuple, half.tolist())) for half in OFFSETS)
    self_even, self_odd = np.argwhere(OFFSETS == 0).tolist()
    self_place = self_even[2]
    own_side = (member == jnp.where(owner % 2 == 0, self_even[1], self_odd[1])).astype(jnp.int32)[None]
    tile_shape = jax.ShapeDtypeStruct((block_size, block_size), f32)
    tiles_shape = jax.ShapeDtypeStruct((PLACES, block_size, block_size), f32)
    tile_bytes = block_size * block_size * 4

    slots, old = pl.pallas_call(
        functools.partial(pick_kernel, rows, table),
        name="pick",
        out_shape=(jax.ShapeDtypeStruct((team * PLACES,), jnp.int32), tiles_shape),
        in_specs=[SMEM, SMEM, SMEM, HBM],
        out_specs=(SMEM, VMEM),
        scratch_shapes=[pltpu.SemaphoreType.DMA((PLACES,))],
        compiler_params=PARAMS,
        cost_estimate=cost(0, 2 * PLACES * tile_bytes),
    )(ids, columns, counts, pltpu.with_memory_space_constraint(weights, pltpu.MemorySpace.HBM))

    full = lax.all_gather(own_dosage, "team", axis=0, tiled=True)
    column = [None] * PLACES
    column[FAR_2] = fetch(full, FAR_2)
    column[NEAR_2] = fetch(full, NEAR_2)
    column[NEAR_1] = fetch(full, NEAR_1)
    column[FAR_1] = fetch(full, FAR_1)
    column[SIDE_2] = permute(column[NEAR_2], beside)
    column[SIDE_1] = permute(column[NEAR_1], beside)

    partial = pl.pallas_call(
        functools.partial(partial_kernel, self_place),
        name="partial",
        out_shape=jax.ShapeDtypeStruct((samples, block_size), f32),
        in_specs=[SMEM] + [VMEM] * (2 + PLACES),
        out_specs=VMEM,
        compiler_params=PARAMS,
        cost_estimate=cost(2 * PLACES * samples * block_size**2, 14 * samples * block_size * 4),
    )(own_side, old, full, *column)
    half = partial + permute(partial, lambda b, t: (b, t ^ 1))
    other = permute(half, lambda b, t: (b, t ^ 2))

    turned = jax.ShapeDtypeStruct((PLACES * block_size, samples), jnp.bfloat16)
    high, low = pl.pallas_call(
        functools.partial(turn_kernel, self_place),
        name="turn",
        out_shape=(turned, turned),
        in_specs=[SMEM] + [VMEM] * (1 + PLACES),
        out_specs=(VMEM, VMEM),
        compiler_params=PARAMS,
        cost_estimate=cost(0, 14 * samples * block_size * 4),
    )(own_side, full, *column)
    near_1, near_2, side, far_1, far_2, y_product = pl.pallas_call(
        tile_kernel,
        name="tiles",
        out_shape=(
            tile_shape,
            tile_shape,
            jax.ShapeDtypeStruct((2, block_size, block_size), f32),
            tile_shape,
            tile_shape,
            jax.ShapeDtypeStruct((samples_here, block_size), f32),
        ),
        in_specs=[SMEM] + [VMEM] * 4,
        out_specs=(VMEM,) * 6,
        compiler_params=PARAMS,
        cost_estimate=cost(2 * PLACES * samples * block_size**2, 14 * samples * block_size * 4),
    )(ids, half, other, high, low)

    handed = permute(side, beside)

    def back(x, k):
        return permute(x, lambda b, t: partner(b, t, k))

    got_far_2 = back(far_2, FAR_2)
    got_far_1 = back(far_1, FAR_1)
    got_2 = back(jnp.stack([near_2, handed[1]]), NEAR_2)
    got_1 = back(jnp.stack([near_1, handed[0]]), NEAR_1)

    def tiles_of(count):
        return jax.ShapeDtypeStruct((count, block_size, block_size), f32)

    near_tiles = pl.pallas_call(
        functools.partial(update_near_kernel, self_place, samples),
        name="update_near",
        out_shape=tiles_of(4),
        in_specs=[SMEM] + [VMEM] * 6,
        out_specs=VMEM,
        compiler_params=PARAMS,
        cost_estimate=cost(0, 16 * tile_bytes),
    )(own_side, old, near_1, near_2, side, got_1, got_2)
    far_tiles, all_tiles = pl.pallas_call(
        functools.partial(update_far_kernel, samples),
        name="update_far",
        out_shape=(tiles_of(2), tiles_of(PLACES)),
        in_specs=[VMEM] * 6,
        out_specs=(VMEM, VMEM),
        compiler_params=PARAMS,
        cost_estimate=cost(0, 16 * tile_bytes),
    )(old, far_1, far_2, got_far_1, got_far_2, near_tiles)

    def chip(b, t):
        return b, t ^ 2

    def core(b, t):
        return b, t ^ 1

    near_across = permute(near_tiles, chip)
    far_across = permute(far_tiles, chip)
    mate = permute(all_tiles, core)
    near_last = permute(near_across, core)
    far_last = permute(far_across, core)

    new_omega = pl.pallas_call(
        blank_kernel,
        name="blank",
        out_shape=tiles_of(slot_count),
        in_specs=[SMEM],
        out_specs=HBM,
        scratch_shapes=[
            pltpu.VMEM((block_size, block_size), f32),
            pltpu.SemaphoreType.DMA((slot_count,)),
        ],
        compiler_params=PARAMS,
        cost_estimate=cost(0, PLACES * tile_bytes),
    )(counts)

    def place(into, *given):
        groups = tuple((j, places) for j, places, _ in given)
        count = sum(len(places) for _, places in groups)
        n = len(groups)
        return pl.pallas_call(
            functools.partial(place_kernel, groups),
            out_shape=tiles_of(slot_count),
            in_specs=[SMEM] * 2 + [VMEM] * n + [HBM],
            out_specs=HBM,
            input_output_aliases={2 + n: 0},
            scratch_shapes=[pltpu.SemaphoreType.DMA((count,))],
            compiler_params=PARAMS,
            cost_estimate=cost(0, 2 * count * tile_bytes),
        )(slots, ids, *(tiles for _, _, tiles in given), into)

    every = tuple(range(PLACES))
    new_omega = place(new_omega, (0, every, all_tiles), (1, every, mate))
    new_omega = place(new_omega, (2, NEAR_PLACES, near_across), (2, FAR_PLACES, far_across))
    new_omega = place(new_omega, (3, NEAR_PLACES, near_last), (3, FAR_PLACES, far_last))
    return (new_omega[None], y_product[None])


def solution(mesh):
    return jax.shard_map(
        step,
        mesh=mesh,
        in_specs=(P("blk", None, None, None), P("blk", "team", None), P("blk", None), P("blk")),
        out_specs=(P("blk", None, None, None), P("blk", "team", None)),
        check_vma=False,
    )
```

```python
import functools

import jax
import jax.numpy as jnp
import numpy as np
from jax import lax
from jax.experimental import pallas as pl
from jax.experimental.pallas import tpu as pltpu
from jax.sharding import PartitionSpec as P


step_size = 0.1
penalty = 0.05


AXES = ("blk", "team")
NEAR_1, NEAR_2, SIDE_1, SIDE_2, FAR_1, FAR_2 = range(6)
PLACES = 6
NEAR = ((2, 8), (4, 6))
FAR = ((51, 0), (25, 38))


def offsets(near, far):
    table = np.zeros((2, 4, PLACES), int)
    for parity in range(2):
        for t in range(4):
            sign = 1 - 2 * (t % 2)
            for i in range(2):
                near_by = sign * near[t // 2][i]
                side = near_by + 1 - 2 * parity
                distant = sign * far[t // 2][i]
                if distant == 0:
                    distant = 1 - 2 * parity if parity == t % 2 else 64
                table[parity, t, i] = near_by
                table[parity, t, 2 + i] = 0 if abs(side) == 9 else side
                table[parity, t, 4 + i] = distant
    return table


OFFSETS = offsets(NEAR, FAR)
VMEM = pl.BlockSpec(memory_space=pltpu.VMEM)
SMEM = pl.BlockSpec(memory_space=pltpu.SMEM)
HBM = pl.BlockSpec(memory_space=pltpu.MemorySpace.HBM)


def split(x):
    high = x.astype(jnp.bfloat16)
    return high, (x - high.astype(jnp.float32)).astype(jnp.bfloat16)


def dot3(a, b, dims):
    def one(x, y):
        return lax.dot_general(x, y, (dims, ((), ())), preferred_element_type=jnp.float32)

    return one(a[0], b[0]) + (one(a[0], b[1]) + one(a[1], b[0]))


def pick_kernel(rows, offset_table, ids, columns, counts, omega, slots, old, sems):
    owner, member = ids[0], ids[1]
    count = counts[0]
    parity = lax.rem(owner, 2)
    choices = np.mod(np.array(offset_table), rows).reshape(2, -1)
    total = choices.shape[1]
    slot_count = columns.shape[1]
    wanted = [jnp.where(parity == 0, int(choices[0, i]), int(choices[1, i])) for i in range(total)]
    for i in range(total):
        slots[i] = -1

    def match(s, carry):
        offset = lax.rem(columns[0, s] - owner + rows, rows)
        for i in range(total):

            @pl.when(wanted[i] == offset)
            def _():
                slots[i] = s

        return carry

    lax.fori_loop(0, jnp.minimum(count, slot_count), match, 0)
    for k in range(PLACES):
        slot = slots[member * PLACES + k]

        @pl.when(slot >= 0)
        def _():
            pltpu.make_async_copy(omega.at[slot], old.at[k], sems.at[k]).start()

        @pl.when(slot < 0)
        def _():
            old[k] = jnp.zeros(old.shape[1:], jnp.float32)

    for k in range(PLACES):
        slot = slots[member * PLACES + k]

        @pl.when(slot >= 0)
        def _():
            pltpu.make_async_copy(omega.at[slot], old.at[k], sems.at[k]).wait()


def partial_kernel(self_place, own_side, old, full, *refs):
    column, out = refs[:PLACES], refs[PLACES]
    total = jnp.zeros(out.shape, jnp.float32)
    for k in range(PLACES):
        x = column[k][...]
        if k == self_place:
            x = jnp.where(own_side[0] == 1, full[...], x)
        total = total + dot3(split(x), split(old[k]), ((1,), (1,)))
    out[...] = total


def turn_kernel(self_place, own_side, full, *refs):
    column, (high, low) = refs[:PLACES], refs[PLACES:]
    block_size = full.shape[1]
    for k in range(PLACES):
        x = column[k][...]
        if k == self_place:
            x = jnp.where(own_side[0] == 1, full[...], x)
        here = pl.ds(k * block_size, block_size)
        high[here, :], low[here, :] = split(x.T)


def tile_kernel(ids, half, other, high, low, *outs):
    near_1, near_2, side, far_1, far_2, y_out = outs
    samples_here, block_size = y_out.shape
    product_high, product_low = split(half[...] + other[...])

    def one(x, y):
        return jnp.dot(x, y, preferred_element_type=jnp.float32)

    both = one(high[...], jnp.concatenate([product_high, product_low], axis=1))
    rest = one(low[...], product_high)
    tiles = both[:, :block_size] + (both[:, block_size:] + rest)
    for k in range(PLACES):
        tile = tiles[k * block_size : (k + 1) * block_size]
        if k in (SIDE_1, SIDE_2):
            side[k - SIDE_1] = tile
        else:
            {NEAR_1: near_1, NEAR_2: near_2, FAR_1: far_1, FAR_2: far_2}[k][...] = tile
    start = pl.multiple_of(ids[1] * samples_here, samples_here)
    y_out[...] = half[pl.ds(start, samples_here), :] + other[pl.ds(start, samples_here), :]


def update(before, ours, theirs, samples, corner=None):
    grad = (ours.T + theirs) / (2.0 * samples)
    if corner is not None:
        grad = grad - jnp.where(corner, 1.0 / jnp.where(corner, before, 1.0), 0.0)
    moved = before - step_size * grad
    size = jnp.maximum(jnp.abs(moved) - step_size * penalty, 0.0)
    shrunk = jnp.where(moved < 0.0, -size, size)
    return shrunk if corner is None else jnp.where(corner, moved, shrunk)


def update_far_kernel(samples, old, far_1, far_2, got_1, got_2, near, far, every):
    far[0] = update(old[FAR_1], far_1[...], got_1[...], samples)
    far[1] = update(old[FAR_2], far_2[...], got_2[...], samples)
    for k in NEAR_PLACES:
        every[k] = near[k]
    for i, k in enumerate(FAR_PLACES):
        every[k] = far[i]


def update_near_kernel(self_place, samples, own_side, old, near_1, near_2, side, got_1, got_2, out):
    on_self = own_side[0] == 1
    shape = out.shape[1:]
    unit = lax.broadcasted_iota(jnp.int32, shape, 0) == lax.broadcasted_iota(jnp.int32, shape, 1)
    corner = jnp.logical_and(unit, on_self)
    ours = [near_1[...], near_2[...], side[0], side[1]]
    theirs = [got_1[0], got_2[0], got_1[1], got_2[1]]
    for k in NEAR_PLACES:
        if k == self_place:
            given = jnp.where(on_self, ours[k], theirs[k])
            out[k] = update(old[k], ours[k], given, samples, corner)
        else:
            out[k] = update(old[k], ours[k], theirs[k], samples)


NEAR_PLACES = (NEAR_1, NEAR_2, SIDE_1, SIDE_2)
FAR_PLACES = (FAR_1, FAR_2)


def blank_kernel(counts, out, zero, sems):
    zero[...] = jnp.zeros(zero.shape, jnp.float32)
    slot_count = out.shape[0]
    first = jnp.clip(counts[0], 0, slot_count)

    @pl.loop(first, slot_count)
    def _(s):
        pltpu.make_async_copy(zero, out.at[s], sems.at[s]).start()

    @pl.loop(first, slot_count)
    def _(s):
        pltpu.make_async_copy(zero, out.at[s], sems.at[s]).wait()


def place_kernel(groups, slots, ids, *refs):
    out, sems = refs[len(groups) + 1 :]
    found = []
    for (j, places), tiles in zip(groups, refs):
        for i, k in enumerate(places):
            slot = slots[lax.bitwise_xor(ids[1], j) * PLACES + k]
            copy = pltpu.make_async_copy(
                tiles.at[i], out.at[jnp.maximum(slot, 0)], sems.at[len(found)]
            )
            found.append((slot >= 0, copy))
    for condition, copy in found:
        pl.when(condition)(copy.start)
    for condition, copy in found:
        pl.when(condition)(copy.wait)


PARAMS = pltpu.CompilerParams(vmem_limit_bytes=8 * 2**20)


def cost(flops, nbytes):
    return pl.CostEstimate(flops=flops, bytes_accessed=nbytes, transcendentals=0)


def step(omega, dosage, columns, counts):
    weights = omega[0]
    own_dosage = dosage[0]
    slot_count, block_size = weights.shape[:2]
    samples_here = own_dosage.shape[0]
    owner = lax.axis_index("blk")
    member = lax.axis_index("team")
    rows = lax.axis_size("blk")
    team = lax.axis_size("team")
    samples = samples_here * team
    f32 = jnp.float32

    def permute(x, target):
        pairs = []
        for b in range(rows):
            for t in range(team):
                found = target(b, t)
                if found is not None:
                    pairs.append((b * team + t, (found[0] % rows) * team + found[1]))
        return lax.ppermute(x, AXES, pairs)

    def partner(b, t, k):
        there = b + OFFSETS[b % 2, t, k]
        found = [
            u for u in range(team) if (OFFSETS[there % 2, u, k] + OFFSETS[b % 2, t, k]) % rows == 0
        ]
        if k in (NEAR_1, NEAR_2) and not 0 <= there < rows:
            return None
        return there, found[0]

    def fetch(x, k):
        source = {}
        for b in range(rows):
            for t in range(team):
                found = partner(b, t, k)
                if found is not None:
                    source[found[0] % rows, found[1]] = (b, t)
        return permute(x, lambda b, t: source.get((b, t)))

    def beside(b, t):
        return b ^ 1, t

    ids = jnp.stack([owner, member]).astype(jnp.int32)
    table = tuple(tuple(map(tuple, half.tolist())) for half in OFFSETS)
    self_even, self_odd = np.argwhere(OFFSETS == 0).tolist()
    self_place = self_even[2]
    own_side = (member == jnp.where(owner % 2 == 0, self_even[1], self_odd[1])).astype(jnp.int32)[None]
    tile_shape = jax.ShapeDtypeStruct((block_size, block_size), f32)
    tiles_shape = jax.ShapeDtypeStruct((PLACES, block_size, block_size), f32)
    tile_bytes = block_size * block_size * 4

    slots, old = pl.pallas_call(
        functools.partial(pick_kernel, rows, table),
        name="pick",
        out_shape=(jax.ShapeDtypeStruct((team * PLACES,), jnp.int32), tiles_shape),
        in_specs=[SMEM, SMEM, SMEM, HBM],
        out_specs=(SMEM, VMEM),
        scratch_shapes=[pltpu.SemaphoreType.DMA((PLACES,))],
        compiler_params=PARAMS,
        cost_estimate=cost(0, 2 * PLACES * tile_bytes),
    )(ids, columns, counts, pltpu.with_memory_space_constraint(weights, pltpu.MemorySpace.HBM))

    full = lax.all_gather(own_dosage, "team", axis=0, tiled=True)
    column = [None] * PLACES
    column[FAR_2] = fetch(full, FAR_2)
    column[NEAR_2] = fetch(full, NEAR_2)
    column[NEAR_1] = fetch(full, NEAR_1)
    column[FAR_1] = fetch(full, FAR_1)
    column[SIDE_2] = permute(column[NEAR_2], beside)
    column[SIDE_1] = permute(column[NEAR_1], beside)

    partial = pl.pallas_call(
        functools.partial(partial_kernel, self_place),
        name="partial",
        out_shape=jax.ShapeDtypeStruct((samples, block_size), f32),
        in_specs=[SMEM] + [VMEM] * (2 + PLACES),
        out_specs=VMEM,
        compiler_params=PARAMS,
        cost_estimate=cost(2 * PLACES * samples * block_size**2, 14 * samples * block_size * 4),
    )(own_side, old, full, *column)
    half = partial + permute(partial, lambda b, t: (b, t ^ 1))
    other = permute(half, lambda b, t: (b, t ^ 2))

    turned = jax.ShapeDtypeStruct((PLACES * block_size, samples), jnp.bfloat16)
    high, low = pl.pallas_call(
        functools.partial(turn_kernel, self_place),
        name="turn",
        out_shape=(turned, turned),
        in_specs=[SMEM] + [VMEM] * (1 + PLACES),
        out_specs=(VMEM, VMEM),
        compiler_params=PARAMS,
        cost_estimate=cost(0, 14 * samples * block_size * 4),
    )(own_side, full, *column)
    near_1, near_2, side, far_1, far_2, y_product = pl.pallas_call(
        tile_kernel,
        name="tiles",
        out_shape=(
            tile_shape,
            tile_shape,
            jax.ShapeDtypeStruct((2, block_size, block_size), f32),
            tile_shape,
            tile_shape,
            jax.ShapeDtypeStruct((samples_here, block_size), f32),
        ),
        in_specs=[SMEM] + [VMEM] * 4,
        out_specs=(VMEM,) * 6,
        compiler_params=PARAMS,
        cost_estimate=cost(2 * PLACES * samples * block_size**2, 14 * samples * block_size * 4),
    )(ids, half, other, high, low)

    handed = permute(side, beside)

    def back(x, k):
        return permute(x, lambda b, t: partner(b, t, k))

    got_far_2 = back(far_2, FAR_2)
    got_far_1 = back(far_1, FAR_1)
    got_2 = back(jnp.stack([near_2, handed[1]]), NEAR_2)
    got_1 = back(jnp.stack([near_1, handed[0]]), NEAR_1)

    def tiles_of(count):
        return jax.ShapeDtypeStruct((count, block_size, block_size), f32)

    near_tiles = pl.pallas_call(
        functools.partial(update_near_kernel, self_place, samples),
        name="update_near",
        out_shape=tiles_of(4),
        in_specs=[SMEM] + [VMEM] * 6,
        out_specs=VMEM,
        compiler_params=PARAMS,
        cost_estimate=cost(0, 16 * tile_bytes),
    )(own_side, old, near_1, near_2, side, got_1, got_2)
    far_tiles, all_tiles = pl.pallas_call(
        functools.partial(update_far_kernel, samples),
        name="update_far",
        out_shape=(tiles_of(2), tiles_of(PLACES)),
        in_specs=[VMEM] * 6,
        out_specs=(VMEM, VMEM),
        compiler_params=PARAMS,
        cost_estimate=cost(0, 16 * tile_bytes),
    )(old, far_1, far_2, got_far_1, got_far_2, near_tiles)

    def chip(b, t):
        return b, t ^ 2

    def core(b, t):
        return b, t ^ 1

    near_across = permute(near_tiles, chip)
    far_across = permute(far_tiles, chip)
    mate = permute(all_tiles, core)
    near_last = permute(near_across, core)
    far_last = permute(far_across, core)

    new_omega = pl.pallas_call(
        blank_kernel,
        name="blank",
        out_shape=tiles_of(slot_count),
        in_specs=[SMEM],
        out_specs=HBM,
        scratch_shapes=[
            pltpu.VMEM((block_size, block_size), f32),
            pltpu.SemaphoreType.DMA((slot_count,)),
        ],
        compiler_params=PARAMS,
        cost_estimate=cost(0, PLACES * tile_bytes),
    )(counts)

    def place(into, *given):
        groups = tuple((j, places) for j, places, _ in given)
        count = sum(len(places) for _, places in groups)
        n = len(groups)
        return pl.pallas_call(
            functools.partial(place_kernel, groups),
            out_shape=tiles_of(slot_count),
            in_specs=[SMEM] * 2 + [VMEM] * n + [HBM],
            out_specs=HBM,
            input_output_aliases={2 + n: 0},
            scratch_shapes=[pltpu.SemaphoreType.DMA((count,))],
            compiler_params=PARAMS,
            cost_estimate=cost(0, 2 * count * tile_bytes),
        )(slots, ids, *(tiles for _, _, tiles in given), into)

    every = tuple(range(PLACES))
    new_omega = place(new_omega, (0, every, all_tiles), (1, every, mate))
    new_omega = place(new_omega, (2, NEAR_PLACES, near_across), (2, FAR_PLACES, far_across))
    new_omega = place(new_omega, (3, NEAR_PLACES, near_last), (3, FAR_PLACES, far_last))
    return (new_omega[None], y_product[None])


def solution(mesh):
    return jax.shard_map(
        step,
        mesh=mesh,
        in_specs=(P("blk", None, None, None), P("blk", "team", None), P("blk", None), P("blk")),
        out_specs=(P("blk", None, None, None), P("blk", "team", None)),
        check_vma=False,
    )
```

```python
import functools

import jax
import jax.numpy as jnp
import numpy as np
from jax import lax
from jax.experimental import pallas as pl
from jax.experimental.pallas import tpu as pltpu
from jax.sharding import PartitionSpec as P


step_size = 0.1
penalty = 0.05


AXES = ("blk", "team")
NEAR_1, NEAR_2, SIDE_1, SIDE_2, FAR_1, FAR_2 = range(6)
PLACES = 6
NEAR = ((2, 6), (4, 8))
FAR = ((51, 0), (25, 38))


def offsets(near, far):
    table = np.zeros((2, 4, PLACES), int)
    for parity in range(2):
        for t in range(4):
            sign = 1 - 2 * (t % 2)
            for i in range(2):
                near_by = sign * near[t // 2][i]
                side = near_by + 1 - 2 * parity
                distant = sign * far[t // 2][i]
                if distant == 0:
                    distant = 1 - 2 * parity if parity == t % 2 else 64
                table[parity, t, i] = near_by
                table[parity, t, 2 + i] = 0 if abs(side) == 9 else side
                table[parity, t, 4 + i] = distant
    return table


OFFSETS = offsets(NEAR, FAR)
VMEM = pl.BlockSpec(memory_space=pltpu.VMEM)
SMEM = pl.BlockSpec(memory_space=pltpu.SMEM)
HBM = pl.BlockSpec(memory_space=pltpu.MemorySpace.HBM)


def split(x):
    high = x.astype(jnp.bfloat16)
    return high, (x - high.astype(jnp.float32)).astype(jnp.bfloat16)


def dot3(a, b, dims):
    def one(x, y):
        return lax.dot_general(x, y, (dims, ((), ())), preferred_element_type=jnp.float32)

    return one(a[0], b[0]) + (one(a[0], b[1]) + one(a[1], b[0]))


def pick_kernel(rows, offset_table, ids, columns, counts, omega, slots, old, sems):
    owner, member = ids[0], ids[1]
    count = counts[0]
    parity = lax.rem(owner, 2)
    choices = np.mod(np.array(offset_table), rows).reshape(2, -1)
    total = choices.shape[1]
    slot_count = columns.shape[1]
    wanted = [jnp.where(parity == 0, int(choices[0, i]), int(choices[1, i])) for i in range(total)]
    for i in range(total):
        slots[i] = -1

    def match(s, carry):
        offset = lax.rem(columns[0, s] - owner + rows, rows)
        for i in range(total):

            @pl.when(wanted[i] == offset)
            def _():
                slots[i] = s

        return carry

    lax.fori_loop(0, jnp.minimum(count, slot_count), match, 0)
    for k in range(PLACES):
        slot = slots[member * PLACES + k]

        @pl.when(slot >= 0)
        def _():
            pltpu.make_async_copy(omega.at[slot], old.at[k], sems.at[k]).start()

        @pl.when(slot < 0)
        def _():
            old[k] = jnp.zeros(old.shape[1:], jnp.float32)

    for k in range(PLACES):
        slot = slots[member * PLACES + k]

        @pl.when(slot >= 0)
        def _():
            pltpu.make_async_copy(omega.at[slot], old.at[k], sems.at[k]).wait()


def partial_kernel(self_place, own_side, old, full, *refs):
    column, out = refs[:PLACES], refs[PLACES]
    total = jnp.zeros(out.shape, jnp.float32)
    for k in range(PLACES):
        x = column[k][...]
        if k == self_place:
            x = jnp.where(own_side[0] == 1, full[...], x)
        total = total + dot3(split(x), split(old[k]), ((1,), (1,)))
    out[...] = total


def turn_kernel(self_place, own_side, full, *refs):
    column, (high, low) = refs[:PLACES], refs[PLACES:]
    block_size = full.shape[1]
    for k in range(PLACES):
        x = column[k][...]
        if k == self_place:
            x = jnp.where(own_side[0] == 1, full[...], x)
        here = pl.ds(k * block_size, block_size)
        high[here, :], low[here, :] = split(x.T)


def tile_kernel(ids, own, mate, across, both_ways, high, low, *outs):
    near_1, near_2, side, far_1, far_2, y_out = outs
    samples_here, block_size = y_out.shape
    product_high, product_low = split((own[...] + mate[...]) + (across[...] + both_ways[...]))

    def one(x, y):
        return jnp.dot(x, y, preferred_element_type=jnp.float32)

    both = one(high[...], jnp.concatenate([product_high, product_low], axis=1))
    rest = one(low[...], product_high)
    tiles = both[:, :block_size] + (both[:, block_size:] + rest)
    for k in range(PLACES):
        tile = tiles[k * block_size : (k + 1) * block_size]
        if k in (SIDE_1, SIDE_2):
            side[k - SIDE_1] = tile
        else:
            {NEAR_1: near_1, NEAR_2: near_2, FAR_1: far_1, FAR_2: far_2}[k][...] = tile
    start = pl.multiple_of(ids[1] * samples_here, samples_here)
    here = (pl.ds(start, samples_here), slice(None))
    y_out[...] = (own[here] + mate[here]) + (across[here] + both_ways[here])


def update(before, ours, theirs, samples, corner=None):
    grad = (ours.T + theirs) / (2.0 * samples)
    if corner is not None:
        grad = grad - jnp.where(corner, 1.0 / jnp.where(corner, before, 1.0), 0.0)
    moved = before - step_size * grad
    size = jnp.maximum(jnp.abs(moved) - step_size * penalty, 0.0)
    shrunk = jnp.where(moved < 0.0, -size, size)
    return shrunk if corner is None else jnp.where(corner, moved, shrunk)


def update_far_kernel(samples, old, far_1, far_2, got_1, got_2, near, far, every):
    far[0] = update(old[FAR_1], far_1[...], got_1[...], samples)
    far[1] = update(old[FAR_2], far_2[...], got_2[...], samples)
    for k in NEAR_PLACES:
        every[k] = near[k]
    for i, k in enumerate(FAR_PLACES):
        every[k] = far[i]


def update_near_kernel(self_place, samples, own_side, old, near_1, near_2, side, got_1, got_2, out):
    on_self = own_side[0] == 1
    shape = out.shape[1:]
    unit = lax.broadcasted_iota(jnp.int32, shape, 0) == lax.broadcasted_iota(jnp.int32, shape, 1)
    corner = jnp.logical_and(unit, on_self)
    ours = [near_1[...], near_2[...], side[0], side[1]]
    theirs = [got_1[0], got_2[0], got_1[1], got_2[1]]
    for k in NEAR_PLACES:
        if k == self_place:
            given = jnp.where(on_self, ours[k], theirs[k])
            out[k] = update(old[k], ours[k], given, samples, corner)
        else:
            out[k] = update(old[k], ours[k], theirs[k], samples)


NEAR_PLACES = (NEAR_1, NEAR_2, SIDE_1, SIDE_2)
FAR_PLACES = (FAR_1, FAR_2)


def blank_kernel(counts, out, zero, sems):
    zero[...] = jnp.zeros(zero.shape, jnp.float32)
    slot_count = out.shape[0]
    first = jnp.clip(counts[0], 0, slot_count)

    @pl.loop(first, slot_count)
    def _(s):
        pltpu.make_async_copy(zero, out.at[s], sems.at[s]).start()

    @pl.loop(first, slot_count)
    def _(s):
        pltpu.make_async_copy(zero, out.at[s], sems.at[s]).wait()


def place_kernel(groups, extra, slots, ids, *refs):
    n = len(groups)
    if extra:
        rows_in, _, out, rows_out, sems, rows_sem = refs[n:]
        rows_copy = pltpu.make_async_copy(rows_in, rows_out, rows_sem)
        rows_copy.start()
    else:
        _, out, sems = refs[n:]
    found = []
    for (j, places), tiles in zip(groups, refs):
        for i, k in enumerate(places):
            slot = slots[lax.bitwise_xor(ids[1], j) * PLACES + k]
            copy = pltpu.make_async_copy(
                tiles.at[i], out.at[jnp.maximum(slot, 0)], sems.at[len(found)]
            )
            found.append((slot >= 0, copy))
    for condition, copy in found:
        pl.when(condition)(copy.start)
    for condition, copy in found:
        pl.when(condition)(copy.wait)
    if extra:
        rows_copy.wait()


PARAMS = pltpu.CompilerParams(vmem_limit_bytes=8 * 2**20)


def cost(flops, nbytes):
    return pl.CostEstimate(flops=flops, bytes_accessed=nbytes, transcendentals=0)


def step(omega, dosage, columns, counts):
    weights = omega[0]
    own_dosage = dosage[0]
    slot_count, block_size = weights.shape[:2]
    samples_here = own_dosage.shape[0]
    owner = lax.axis_index("blk")
    member = lax.axis_index("team")
    rows = lax.axis_size("blk")
    team = lax.axis_size("team")
    samples = samples_here * team
    f32 = jnp.float32

    def permute(x, target):
        pairs = []
        for b in range(rows):
            for t in range(team):
                found = target(b, t)
                if found is not None:
                    pairs.append((b * team + t, (found[0] % rows) * team + found[1]))
        return lax.ppermute(x, AXES, pairs)

    def partner(b, t, k):
        there = b + OFFSETS[b % 2, t, k]
        found = [
            u for u in range(team) if (OFFSETS[there % 2, u, k] + OFFSETS[b % 2, t, k]) % rows == 0
        ]
        if k in (NEAR_1, NEAR_2) and not 0 <= there < rows:
            return None
        return there, found[0]

    def fetch(x, k):
        source = {}
        for b in range(rows):
            for t in range(team):
                found = partner(b, t, k)
                if found is not None:
                    source[found[0] % rows, found[1]] = (b, t)
        return permute(x, lambda b, t: source.get((b, t)))

    def beside(b, t):
        return b ^ 1, t

    ids = jnp.stack([owner, member]).astype(jnp.int32)
    table = tuple(tuple(map(tuple, half.tolist())) for half in OFFSETS)
    self_even, self_odd = np.argwhere(OFFSETS == 0).tolist()
    self_place = self_even[2]
    own_side = (member == jnp.where(owner % 2 == 0, self_even[1], self_odd[1])).astype(jnp.int32)[None]
    tile_shape = jax.ShapeDtypeStruct((block_size, block_size), f32)
    tiles_shape = jax.ShapeDtypeStruct((PLACES, block_size, block_size), f32)
    tile_bytes = block_size * block_size * 4

    slots, old = pl.pallas_call(
        functools.partial(pick_kernel, rows, table),
        name="pick",
        out_shape=(jax.ShapeDtypeStruct((team * PLACES,), jnp.int32), tiles_shape),
        in_specs=[SMEM, SMEM, SMEM, HBM],
        out_specs=(SMEM, VMEM),
        scratch_shapes=[pltpu.SemaphoreType.DMA((PLACES,))],
        compiler_params=PARAMS,
        cost_estimate=cost(0, 2 * PLACES * tile_bytes),
    )(ids, columns, counts, pltpu.with_memory_space_constraint(weights, pltpu.MemorySpace.HBM))

    full = lax.all_gather(own_dosage, "team", axis=0, tiled=True)
    column = [None] * PLACES
    column[FAR_2] = fetch(full, FAR_2)
    column[NEAR_2] = fetch(full, NEAR_2)
    column[NEAR_1] = fetch(full, NEAR_1)
    column[FAR_1] = fetch(full, FAR_1)
    column[SIDE_2] = permute(column[NEAR_2], beside)
    column[SIDE_1] = permute(column[NEAR_1], beside)

    partial = pl.pallas_call(
        functools.partial(partial_kernel, self_place),
        name="partial",
        out_shape=jax.ShapeDtypeStruct((samples, block_size), f32),
        in_specs=[SMEM] + [VMEM] * (2 + PLACES),
        out_specs=VMEM,
        compiler_params=PARAMS,
        cost_estimate=cost(2 * PLACES * samples * block_size**2, 14 * samples * block_size * 4),
    )(own_side, old, full, *column)
    products = [
        partial,
        permute(partial, lambda b, t: (b, t ^ 1)),
        permute(partial, lambda b, t: (b, t ^ 2)),
        permute(partial, lambda b, t: (b, t ^ 3)),
    ]

    turned = jax.ShapeDtypeStruct((PLACES * block_size, samples), jnp.bfloat16)
    high, low = pl.pallas_call(
        functools.partial(turn_kernel, self_place),
        name="turn",
        out_shape=(turned, turned),
        in_specs=[SMEM] + [VMEM] * (1 + PLACES),
        out_specs=(VMEM, VMEM),
        compiler_params=PARAMS,
        cost_estimate=cost(0, 14 * samples * block_size * 4),
    )(own_side, full, *column)
    near_1, near_2, side, far_1, far_2, own_rows = pl.pallas_call(
        tile_kernel,
        name="tiles",
        out_shape=(
            tile_shape,
            tile_shape,
            jax.ShapeDtypeStruct((2, block_size, block_size), f32),
            tile_shape,
            tile_shape,
            jax.ShapeDtypeStruct((samples_here, block_size), f32),
        ),
        in_specs=[SMEM] + [VMEM] * 6,
        out_specs=(VMEM,) * 6,
        compiler_params=PARAMS,
        cost_estimate=cost(2 * PLACES * samples * block_size**2, 14 * samples * block_size * 4),
    )(ids, *products, high, low)

    handed = permute(side, beside)

    def back(x, k):
        return permute(x, lambda b, t: partner(b, t, k))

    got_far_2 = back(far_2, FAR_2)
    got_far_1 = back(far_1, FAR_1)
    got_2 = back(jnp.stack([near_2, handed[1]]), NEAR_2)
    got_1 = back(jnp.stack([near_1, handed[0]]), NEAR_1)

    def tiles_of(count):
        return jax.ShapeDtypeStruct((count, block_size, block_size), f32)

    near_tiles = pl.pallas_call(
        functools.partial(update_near_kernel, self_place, samples),
        name="update_near",
        out_shape=tiles_of(4),
        in_specs=[SMEM] + [VMEM] * 6,
        out_specs=VMEM,
        compiler_params=PARAMS,
        cost_estimate=cost(0, 16 * tile_bytes),
    )(own_side, old, near_1, near_2, side, got_1, got_2)
    far_tiles, all_tiles = pl.pallas_call(
        functools.partial(update_far_kernel, samples),
        name="update_far",
        out_shape=(tiles_of(2), tiles_of(PLACES)),
        in_specs=[VMEM] * 6,
        out_specs=(VMEM, VMEM),
        compiler_params=PARAMS,
        cost_estimate=cost(0, 16 * tile_bytes),
    )(old, far_1, far_2, got_far_1, got_far_2, near_tiles)

    def chip(b, t):
        return b, t ^ 2

    def core(b, t):
        return b, t ^ 1

    near_across = permute(near_tiles, chip)
    far_across = permute(far_tiles, chip)
    mate = permute(all_tiles, core)
    near_last = permute(near_across, core)
    far_last = permute(far_across, core)

    new_omega = pl.pallas_call(
        blank_kernel,
        name="blank",
        out_shape=tiles_of(slot_count),
        in_specs=[SMEM],
        out_specs=HBM,
        scratch_shapes=[
            pltpu.VMEM((block_size, block_size), f32),
            pltpu.SemaphoreType.DMA((slot_count,)),
        ],
        compiler_params=PARAMS,
        cost_estimate=cost(0, PLACES * tile_bytes),
    )(counts)

    def place(into, own_rows, *given):
        groups = tuple((j, places) for j, places, _ in given)
        count = sum(len(places) for _, places in groups)
        extra = own_rows is not None
        operands = [tiles for _, _, tiles in given] + ([own_rows] if extra else [])
        n = len(operands)
        rows_shape = jax.ShapeDtypeStruct((samples_here, block_size), f32)
        return pl.pallas_call(
            functools.partial(place_kernel, groups, extra),
            out_shape=(tiles_of(slot_count), rows_shape) if extra else tiles_of(slot_count),
            in_specs=[SMEM] * 2 + [VMEM] * n + [HBM],
            out_specs=(HBM, HBM) if extra else HBM,
            input_output_aliases={2 + n: 0},
            scratch_shapes=[pltpu.SemaphoreType.DMA((count,))]
            + ([pltpu.SemaphoreType.DMA] if extra else []),
            compiler_params=PARAMS,
            cost_estimate=cost(0, 2 * count * tile_bytes),
        )(slots, ids, *operands, into)

    every = tuple(range(PLACES))
    new_omega, y_product = place(
        new_omega,
        own_rows,
        (0, every, all_tiles),
        (1, every, mate),
        (2, NEAR_PLACES, near_across),
        (2, FAR_PLACES, far_across),
    )
    new_omega = place(new_omega, None, (3, NEAR_PLACES, near_last), (3, FAR_PLACES, far_last))
    return (new_omega[None], y_product[None])


def solution(mesh):
    return jax.shard_map(
        step,
        mesh=mesh,
        in_specs=(P("blk", None, None, None), P("blk", "team", None), P("blk", None), P("blk")),
        out_specs=(P("blk", None, None, None), P("blk", "team", None)),
        check_vma=False,
    )
```

```python
import functools

import jax
import jax.numpy as jnp
import numpy as np
from jax import lax
from jax.experimental import pallas as pl
from jax.experimental.pallas import tpu as pltpu
from jax.sharding import PartitionSpec as P


step_size = 0.1
penalty = 0.05


AXES = ("blk", "team")
NEAR_1, NEAR_2, SIDE_1, SIDE_2, FAR_1, FAR_2 = range(6)
PLACES = 6
NEAR = ((2, 6), (-4, -8))
FAR = ((51, 0), (25, 38))


def offsets(near, far):
    table = np.zeros((2, 4, PLACES), int)
    for parity in range(2):
        for t in range(4):
            sign = 1 - 2 * (t % 2)
            for i in range(2):
                near_by = sign * near[t // 2][i]
                side = near_by + 1 - 2 * parity
                distant = sign * far[t // 2][i]
                if distant == 0:
                    distant = 1 - 2 * parity if parity == t % 2 else 64
                table[parity, t, i] = near_by
                table[parity, t, 2 + i] = 0 if abs(side) == 9 else side
                table[parity, t, 4 + i] = distant
    return table


OFFSETS = offsets(NEAR, FAR)
VMEM = pl.BlockSpec(memory_space=pltpu.VMEM)
SMEM = pl.BlockSpec(memory_space=pltpu.SMEM)
HBM = pl.BlockSpec(memory_space=pltpu.MemorySpace.HBM)


def split(x):
    high = x.astype(jnp.bfloat16)
    return high, (x - high.astype(jnp.float32)).astype(jnp.bfloat16)


def dot3(a, b, dims):
    def one(x, y):
        return lax.dot_general(x, y, (dims, ((), ())), preferred_element_type=jnp.float32)

    return one(a[0], b[0]) + (one(a[0], b[1]) + one(a[1], b[0]))


def pick_kernel(rows, offset_table, ids, columns, counts, omega, slots, old, sems):
    owner, member = ids[0], ids[1]
    count = counts[0]
    parity = lax.rem(owner, 2)
    choices = np.mod(np.array(offset_table), rows).reshape(2, -1)
    total = choices.shape[1]
    slot_count = columns.shape[1]
    wanted = [jnp.where(parity == 0, int(choices[0, i]), int(choices[1, i])) for i in range(total)]
    for i in range(total):
        slots[i] = -1

    def match(s, carry):
        offset = lax.rem(columns[0, s] - owner + rows, rows)
        for i in range(total):

            @pl.when(wanted[i] == offset)
            def _():
                slots[i] = s

        return carry

    lax.fori_loop(0, jnp.minimum(count, slot_count), match, 0)
    for k in range(PLACES):
        slot = slots[member * PLACES + k]

        @pl.when(slot >= 0)
        def _():
            pltpu.make_async_copy(omega.at[slot], old.at[k], sems.at[k]).start()

        @pl.when(slot < 0)
        def _():
            old[k] = jnp.zeros(old.shape[1:], jnp.float32)

    for k in range(PLACES):
        slot = slots[member * PLACES + k]

        @pl.when(slot >= 0)
        def _():
            pltpu.make_async_copy(omega.at[slot], old.at[k], sems.at[k]).wait()


def partial_kernel(self_place, own_side, old, full, *refs):
    column, out = refs[:PLACES], refs[PLACES]
    total = jnp.zeros(out.shape, jnp.float32)
    for k in range(PLACES):
        x = column[k][...]
        if k == self_place:
            x = jnp.where(own_side[0] == 1, full[...], x)
        total = total + dot3(split(x), split(old[k]), ((1,), (1,)))
    out[...] = total


def turn_kernel(self_place, own_side, full, *refs):
    column, (high, low) = refs[:PLACES], refs[PLACES:]
    block_size = full.shape[1]
    for k in range(PLACES):
        x = column[k][...]
        if k == self_place:
            x = jnp.where(own_side[0] == 1, full[...], x)
        here = pl.ds(k * block_size, block_size)
        high[here, :], low[here, :] = split(x.T)


def tile_kernel(ids, half, other, high, low, *outs):
    near_1, near_2, side, far_1, far_2, y_out = outs
    samples_here, block_size = y_out.shape
    product_high, product_low = split(half[...] + other[...])

    def one(x, y):
        return jnp.dot(x, y, preferred_element_type=jnp.float32)

    both = one(high[...], jnp.concatenate([product_high, product_low], axis=1))
    rest = one(low[...], product_high)
    tiles = both[:, :block_size] + (both[:, block_size:] + rest)
    for k in range(PLACES):
        tile = tiles[k * block_size : (k + 1) * block_size]
        if k in (SIDE_1, SIDE_2):
            side[k - SIDE_1] = tile
        else:
            {NEAR_1: near_1, NEAR_2: near_2, FAR_1: far_1, FAR_2: far_2}[k][...] = tile
    start = pl.multiple_of(ids[1] * samples_here, samples_here)
    y_out[...] = half[pl.ds(start, samples_here), :] + other[pl.ds(start, samples_here), :]


def update(before, ours, theirs, samples, corner=None):
    grad = (ours.T + theirs) / (2.0 * samples)
    if corner is not None:
        grad = grad - jnp.where(corner, 1.0 / jnp.where(corner, before, 1.0), 0.0)
    moved = before - step_size * grad
    size = jnp.maximum(jnp.abs(moved) - step_size * penalty, 0.0)
    shrunk = jnp.where(moved < 0.0, -size, size)
    return shrunk if corner is None else jnp.where(corner, moved, shrunk)


def update_far_kernel(samples, old, far_1, far_2, got_1, got_2, near, far, every):
    far[0] = update(old[FAR_1], far_1[...], got_1[...], samples)
    far[1] = update(old[FAR_2], far_2[...], got_2[...], samples)
    for k in NEAR_PLACES:
        every[k] = near[k]
    for i, k in enumerate(FAR_PLACES):
        every[k] = far[i]


def update_near_kernel(self_place, samples, own_side, old, near_1, near_2, side, got_1, got_2, out):
    on_self = own_side[0] == 1
    shape = out.shape[1:]
    unit = lax.broadcasted_iota(jnp.int32, shape, 0) == lax.broadcasted_iota(jnp.int32, shape, 1)
    corner = jnp.logical_and(unit, on_self)
    ours = [near_1[...], near_2[...], side[0], side[1]]
    theirs = [got_1[0], got_2[0], got_1[1], got_2[1]]
    for k in NEAR_PLACES:
        if k == self_place:
            given = jnp.where(on_self, ours[k], theirs[k])
            out[k] = update(old[k], ours[k], given, samples, corner)
        else:
            out[k] = update(old[k], ours[k], theirs[k], samples)


NEAR_PLACES = (NEAR_1, NEAR_2, SIDE_1, SIDE_2)
FAR_PLACES = (FAR_1, FAR_2)


def blank_kernel(counts, out, zero, sems):
    zero[...] = jnp.zeros(zero.shape, jnp.float32)
    slot_count = out.shape[0]
    first = jnp.clip(counts[0], 0, slot_count)

    @pl.loop(first, slot_count)
    def _(s):
        pltpu.make_async_copy(zero, out.at[s], sems.at[s]).start()

    @pl.loop(first, slot_count)
    def _(s):
        pltpu.make_async_copy(zero, out.at[s], sems.at[s]).wait()


def place_kernel(groups, extra, slots, ids, *refs):
    n = len(groups)
    if extra:
        rows_in, _, out, rows_out, sems, rows_sem = refs[n:]
        rows_copy = pltpu.make_async_copy(rows_in, rows_out, rows_sem)
        rows_copy.start()
    else:
        _, out, sems = refs[n:]
    found = []
    for (j, places), tiles in zip(groups, refs):
        for i, k in enumerate(places):
            slot = slots[lax.bitwise_xor(ids[1], j) * PLACES + k]
            copy = pltpu.make_async_copy(
                tiles.at[i], out.at[jnp.maximum(slot, 0)], sems.at[len(found)]
            )
            found.append((slot >= 0, copy))
    for condition, copy in found:
        pl.when(condition)(copy.start)
    for condition, copy in found:
        pl.when(condition)(copy.wait)
    if extra:
        rows_copy.wait()


PARAMS = pltpu.CompilerParams(vmem_limit_bytes=8 * 2**20)


def cost(flops, nbytes):
    return pl.CostEstimate(flops=flops, bytes_accessed=nbytes, transcendentals=0)


def step(omega, dosage, columns, counts):
    weights = omega[0]
    own_dosage = dosage[0]
    slot_count, block_size = weights.shape[:2]
    samples_here = own_dosage.shape[0]
    owner = lax.axis_index("blk")
    member = lax.axis_index("team")
    rows = lax.axis_size("blk")
    team = lax.axis_size("team")
    samples = samples_here * team
    f32 = jnp.float32

    def permute(x, target):
        pairs = []
        for b in range(rows):
            for t in range(team):
                found = target(b, t)
                if found is not None:
                    pairs.append((b * team + t, (found[0] % rows) * team + found[1]))
        return lax.ppermute(x, AXES, pairs)

    def partner(b, t, k):
        there = b + OFFSETS[b % 2, t, k]
        found = [
            u for u in range(team) if (OFFSETS[there % 2, u, k] + OFFSETS[b % 2, t, k]) % rows == 0
        ]
        if k in (NEAR_1, NEAR_2) and not 0 <= there < rows:
            return None
        return there, found[0]

    def fetch(x, k):
        source = {}
        for b in range(rows):
            for t in range(team):
                found = partner(b, t, k)
                if found is not None:
                    source[found[0] % rows, found[1]] = (b, t)
        return permute(x, lambda b, t: source.get((b, t)))

    def beside(b, t):
        return b ^ 1, t

    ids = jnp.stack([owner, member]).astype(jnp.int32)
    table = tuple(tuple(map(tuple, half.tolist())) for half in OFFSETS)
    self_even, self_odd = np.argwhere(OFFSETS == 0).tolist()
    self_place = self_even[2]
    own_side = (member == jnp.where(owner % 2 == 0, self_even[1], self_odd[1])).astype(jnp.int32)[None]
    tile_shape = jax.ShapeDtypeStruct((block_size, block_size), f32)
    tiles_shape = jax.ShapeDtypeStruct((PLACES, block_size, block_size), f32)
    tile_bytes = block_size * block_size * 4

    slots, old = pl.pallas_call(
        functools.partial(pick_kernel, rows, table),
        name="pick",
        out_shape=(jax.ShapeDtypeStruct((team * PLACES,), jnp.int32), tiles_shape),
        in_specs=[SMEM, SMEM, SMEM, HBM],
        out_specs=(SMEM, VMEM),
        scratch_shapes=[pltpu.SemaphoreType.DMA((PLACES,))],
        compiler_params=PARAMS,
        cost_estimate=cost(0, 2 * PLACES * tile_bytes),
    )(ids, columns, counts, pltpu.with_memory_space_constraint(weights, pltpu.MemorySpace.HBM))

    full = lax.all_gather(own_dosage, "team", axis=0, tiled=True)
    column = [None] * PLACES
    column[FAR_2] = fetch(full, FAR_2)
    column[NEAR_2] = fetch(full, NEAR_2)
    column[NEAR_1] = fetch(full, NEAR_1)
    column[FAR_1] = fetch(full, FAR_1)
    column[SIDE_2] = permute(column[NEAR_2], beside)
    column[SIDE_1] = permute(column[NEAR_1], beside)

    partial = pl.pallas_call(
        functools.partial(partial_kernel, self_place),
        name="partial",
        out_shape=jax.ShapeDtypeStruct((samples, block_size), f32),
        in_specs=[SMEM] + [VMEM] * (2 + PLACES),
        out_specs=VMEM,
        compiler_params=PARAMS,
        cost_estimate=cost(2 * PLACES * samples * block_size**2, 14 * samples * block_size * 4),
    )(own_side, old, full, *column)
    half = partial + permute(partial, lambda b, t: (b, t ^ 1))
    other = permute(half, lambda b, t: (b, t ^ 2))

    turned = jax.ShapeDtypeStruct((PLACES * block_size, samples), jnp.bfloat16)
    high, low = pl.pallas_call(
        functools.partial(turn_kernel, self_place),
        name="turn",
        out_shape=(turned, turned),
        in_specs=[SMEM] + [VMEM] * (1 + PLACES),
        out_specs=(VMEM, VMEM),
        compiler_params=PARAMS,
        cost_estimate=cost(0, 14 * samples * block_size * 4),
    )(own_side, full, *column)
    near_1, near_2, side, far_1, far_2, own_rows = pl.pallas_call(
        tile_kernel,
        name="tiles",
        out_shape=(
            tile_shape,
            tile_shape,
            jax.ShapeDtypeStruct((2, block_size, block_size), f32),
            tile_shape,
            tile_shape,
            jax.ShapeDtypeStruct((samples_here, block_size), f32),
        ),
        in_specs=[SMEM] + [VMEM] * 4,
        out_specs=(VMEM,) * 6,
        compiler_params=PARAMS,
        cost_estimate=cost(2 * PLACES * samples * block_size**2, 14 * samples * block_size * 4),
    )(ids, half, other, high, low)

    handed = permute(side, beside)

    def back(x, k):
        return permute(x, lambda b, t: partner(b, t, k))

    got_far_2 = back(far_2, FAR_2)
    got_far_1 = back(far_1, FAR_1)
    got_2 = back(jnp.stack([near_2, handed[1]]), NEAR_2)
    got_1 = back(jnp.stack([near_1, handed[0]]), NEAR_1)

    def tiles_of(count):
        return jax.ShapeDtypeStruct((count, block_size, block_size), f32)

    near_tiles = pl.pallas_call(
        functools.partial(update_near_kernel, self_place, samples),
        name="update_near",
        out_shape=tiles_of(4),
        in_specs=[SMEM] + [VMEM] * 6,
        out_specs=VMEM,
        compiler_params=PARAMS,
        cost_estimate=cost(0, 16 * tile_bytes),
    )(own_side, old, near_1, near_2, side, got_1, got_2)
    far_tiles, all_tiles = pl.pallas_call(
        functools.partial(update_far_kernel, samples),
        name="update_far",
        out_shape=(tiles_of(2), tiles_of(PLACES)),
        in_specs=[VMEM] * 6,
        out_specs=(VMEM, VMEM),
        compiler_params=PARAMS,
        cost_estimate=cost(0, 16 * tile_bytes),
    )(old, far_1, far_2, got_far_1, got_far_2, near_tiles)

    def chip(b, t):
        return b, t ^ 2

    def core(b, t):
        return b, t ^ 1

    near_across = permute(near_tiles, chip)
    far_across = permute(far_tiles, chip)
    mate = permute(all_tiles, core)
    near_last = permute(near_across, core)
    far_last = permute(far_across, core)

    new_omega = pl.pallas_call(
        blank_kernel,
        name="blank",
        out_shape=tiles_of(slot_count),
        in_specs=[SMEM],
        out_specs=HBM,
        scratch_shapes=[
            pltpu.VMEM((block_size, block_size), f32),
            pltpu.SemaphoreType.DMA((slot_count,)),
        ],
        compiler_params=PARAMS,
        cost_estimate=cost(0, PLACES * tile_bytes),
    )(counts)

    def place(into, own_rows, *given):
        groups = tuple((j, places) for j, places, _ in given)
        count = sum(len(places) for _, places in groups)
        extra = own_rows is not None
        operands = [tiles for _, _, tiles in given] + ([own_rows] if extra else [])
        n = len(operands)
        rows_shape = jax.ShapeDtypeStruct((samples_here, block_size), f32)
        return pl.pallas_call(
            functools.partial(place_kernel, groups, extra),
            out_shape=(tiles_of(slot_count), rows_shape) if extra else tiles_of(slot_count),
            in_specs=[SMEM] * 2 + [VMEM] * n + [HBM],
            out_specs=(HBM, HBM) if extra else HBM,
            input_output_aliases={2 + n: 0},
            scratch_shapes=[pltpu.SemaphoreType.DMA((count,))]
            + ([pltpu.SemaphoreType.DMA] if extra else []),
            compiler_params=PARAMS,
            cost_estimate=cost(0, 2 * count * tile_bytes),
        )(slots, ids, *operands, into)

    every = tuple(range(PLACES))
    new_omega, y_product = place(
        new_omega,
        own_rows,
        (0, every, all_tiles),
        (1, every, mate),
        (2, NEAR_PLACES, near_across),
        (2, FAR_PLACES, far_across),
    )
    new_omega = place(new_omega, None, (3, NEAR_PLACES, near_last), (3, FAR_PLACES, far_last))
    return (new_omega[None], y_product[None])


def solution(mesh):
    return jax.shard_map(
        step,
        mesh=mesh,
        in_specs=(P("blk", None, None, None), P("blk", "team", None), P("blk", None), P("blk")),
        out_specs=(P("blk", None, None, None), P("blk", "team", None)),
        check_vma=False,
    )
```
